256 devices in a mesh: dm: 4 (over y), freq: 64 (over z, x, core).
Axes of the slice: x: 4, y: 4, z: 8, core: 2. Of those that a mesh axis runs over, the one named last changes fastest.
Arguments:
- series: float32 [16777216], P(('dm', 'freq')), parts along dimension 0, may hold values from -6 to 6
- kernels: float32 [2, 16, 129], replicated, may hold values from -0.5 to 0.5
- half_widths: int32 [16], replicated, may hold values from 32 to 64, as said below
- sub_rows: int32 [3, 16], replicated, may hold values from 0 to 15
Outputs:
- summed: float32 [16, 8388608], P(None, ('dm', 'freq')), parts along dimension 1
The draws below stay inside these ranges and needn't reach their ends.
There are 4 independent parts, one for each index of `dm`. The reference program is written for one: setup_inputs(seed, part) draws one part's arguments, and reference() takes and returns one part's arrays. A program takes and returns all parts, laid end to end along the dimension named above; an argument that names none is the same for every part. Nothing has to cross between parts.
Inputs may be any that keep to these rules, and one draw needn't show every extreme that they name: Template t's kernel is nonzero only at offsets |j| <= half_widths[t]; some template has half-width exactly 64.
All inputs are finite; a program needn't handle non-finite values.
Results may differ from the reference program's by a relative error of at most 0.000051.
Values sent between devices are 32-bit elements; how exact they have to be, the bound alone decides.
No kernel may reach another device: no remote copies, remote signals or barrier semaphores. Data moves between devices by JAX's collectives and lax.ppermute only.
A program may use at most 128 MiB of HBM per device.

```python
import math
import jax
import jax.numpy as jnp
from jax import lax

SAMPLES = 4194304
TEMPL = 16
MAXHALF = 64


def draw_half_widths(key, part):
    widths = jax.random.randint(jax.random.fold_in(key, 11), (TEMPL,), MAXHALF // 2, MAXHALF + 1, dtype=jnp.int32)
    chosen = jax.random.randint(jax.random.fold_in(key, 12), (), 0, TEMPL, dtype=jnp.int32)
    return jnp.where(jnp.arange(TEMPL, dtype=jnp.int32) == chosen, MAXHALF, widths).astype(jnp.int32)


def plant(array, own_key, least, largest):
    shape = array.shape
    index_at = [jax.random.randint(jax.random.fold_in(own_key, axis), (), 0, shape[axis]) for axis in range(len(shape))]
    array = array.at[tuple(index_at)].set(least)
    longest = shape.index(max(shape))
    index_at[longest] = (index_at[longest] + 1) % shape[longest]
    return array.at[tuple(index_at)].set(largest)


def shard_levels(own_key, dims, split, smallest, largest):
    loudness, own = 1.0, jax.random.fold_in(own_key, 6)
    for axis_at, shards_of in split:
        heights = jnp.exp(jax.random.uniform(jax.random.fold_in(own, axis_at), (shards_of,), jnp.float32, smallest / len(split), largest / len(split)))
        loudness = loudness * jnp.repeat(heights, dims[axis_at] // shards_of).reshape([-1 if axis == axis_at else 1 for axis in range(len(dims))])
    return loudness


def gaussian(stream_key, dims, scale, most, split=(), held_as=jnp.bfloat16):
    level = shard_levels(stream_key, dims, split, -0.22, 0.18) if split else 1.0
    result = jax.random.normal(stream_key, dims, jnp.float32) * scale * level
    return jnp.minimum(jnp.maximum(result, -most), most).astype(held_as)


def setup_inputs(seed: int = 0, part: int = 0) -> dict:
    arg_keys = jax.random.split(jax.random.key(seed), 5)
    part_keys = jax.random.split(jax.random.fold_in(arg_keys[4], part), 5)
    series = gaussian(part_keys[0], (SAMPLES,), 1.0, 6.0, ((0, 64),), jnp.float32)
    kernels = gaussian(arg_keys[1], (2, TEMPL, 2 * MAXHALF + 1), (2 * MAXHALF + 1) ** -0.5, 0.5, (), jnp.float32)
    half_widths = draw_half_widths(jax.random.fold_in(arg_keys[4], 71), part)
    sub_rows = plant(jax.random.randint(arg_keys[3], (3, TEMPL), 0, TEMPL), jax.random.fold_in(arg_keys[3], 1), 0, TEMPL - 1).astype(jnp.int32)
    return dict(series=series, kernels=kernels, half_widths=half_widths, sub_rows=sub_rows)


def masked_taps(kernels, half_widths):
    tap_count = kernels.shape[2]
    half_span = tap_count // 2
    offsets = jnp.abs(jnp.arange(tap_count, dtype=jnp.int32) - half_span)
    inside = offsets[None, :] <= half_widths[:, None]
    return jnp.where(inside[None, :, :], kernels, jnp.zeros_like(kernels))

def reference(series, kernels, half_widths, sub_rows):
    bin_count = SAMPLES // 2
    half_span = MAXHALF
    spectrum = jnp.fft.rfft(series)[:bin_count] / math.sqrt(SAMPLES)
    padded = jnp.concatenate([spectrum, jnp.zeros_like(spectrum)])
    spread = jnp.fft.fft(padded)
    taps = masked_taps(kernels, half_widths)
    filler = jnp.zeros((2 * bin_count - 2 * half_span - 1,), kernels.dtype)

    def one_template(kernel_pair):
        real_taps, imag_taps = kernel_pair
        front_taps = lax.complex(real_taps[half_span::-1], imag_taps[half_span::-1])
        back_taps = lax.complex(real_taps[2 * half_span:half_span:-1], imag_taps[2 * half_span:half_span:-1])
        kernel = jnp.concatenate([front_taps, lax.complex(filler, filler), back_taps])
        response = jnp.fft.ifft(spread * jnp.fft.fft(kernel))[:bin_count]
        return jnp.real(response) * jnp.real(response) + jnp.imag(response) * jnp.imag(response)
    plane = lax.map(one_template, (taps[0], taps[1]))
    positions = jnp.arange(bin_count, dtype=jnp.int32)
    summed = plane
    for harmonic in range(1, 4):
        row_picks = jnp.take(plane, sub_rows[harmonic - 1], axis=0)
        summed = summed + jnp.take(row_picks, harmonic * positions // 4, axis=1)
    return summed
```

```python
import math

import jax
import jax.numpy as jnp
import numpy as np
from jax import lax
from jax.experimental import pallas as pl
from jax.experimental.pallas import tpu as pltpu
from jax.sharding import PartitionSpec as P

SAMPLES = 4194304
TEMPL = 16
MAXHALF = 64
MEMBERS = 64
LANES = 128
ROWS_OUT = 21

highest = lax.Precision.HIGHEST
f32 = jnp.float32
bf16 = jnp.bfloat16

MAIN, HALF2, HALF3, HALF1 = 0, 1, 2, 3
COUNTS = (256, 128, 192, 64)
BASES = (0, 264, 400, 600)
GATHERED = 672
WINDOWS = 640


def unit(product, length):
    angles = np.asarray(product, np.float64) % length * (-2.0 * math.pi / length)
    return np.cos(angles), np.sin(angles)


def first_matrix():
    matrix = np.zeros((128, 128))
    wide = np.arange(128)
    for k0 in range(64):
        real, imag = unit(k0 * wide, 128)
        matrix[2 * k0] = real
        matrix[2 * k0 + 1] = imag
    matrix[1] = unit(64 * wide, 128)[0]
    return matrix.astype(np.float32)


def row_order():
    at = np.arange(256)
    return 4 * (at % 64) + at // 64


def second_matrix():
    q, a = np.arange(256)[:, None], row_order()[None, :]
    real, imag = unit(q * a, 256)
    return np.block([[real, -imag], [imag, real]]).astype(np.float32)


def middle_twiddle():
    q, b = np.arange(256)[:, None], np.arange(128)[None, :]
    real, imag = unit(q * b, 32768)
    return np.stack([real, imag]).astype(np.float32)


def third_matrix():
    c, b = np.arange(72)[:, None], np.arange(128)[None, :]
    real, imag = unit(c * b, 128)
    norm = 1.0 / math.sqrt(SAMPLES)
    return (np.block([[real, -imag], [imag, real]]) * norm).astype(np.float32)


def spread_matrices():
    lane, s = np.arange(128)[:, None], np.arange(128)[None, :]
    one = np.concatenate([lane == 32 * u + s // 4 for u in range(4)], axis=1)
    two = np.concatenate([lane == 64 * u + s // 2 for u in range(2)], axis=1)
    threes = [
        np.concatenate(
            [128 * v + lane == 96 * beta + 3 * s // 4 for beta in (v, v + 1)], axis=1
        )
        for v in range(3)
    ]
    one, two, threes = (np.concatenate([m, m], axis=-2) for m in (one, two, np.stack(threes)))
    return one.astype(bf16), two.astype(bf16), threes.astype(bf16)


def flip_matrix():
    at = np.arange(64)
    return ((64 - at[:, None]) % 64 == at[None, :]).astype(bf16)


def halves(values):
    high = values.astype(bf16)
    return high, (values - high.astype(f32)).astype(bf16)


def first_kernel(matrix_ref, x_ref, out_ref):
    for jj in range(4):
        block = x_ref[pl.ds(jj, 128, stride=4), :]
        out_ref[pl.ds(jj, 128, stride=4), :] = jnp.dot(
            matrix_ref[...], block, precision=highest, preferred_element_type=f32
        )


def spectrum_kernel(
    x_ref, turns_ref, second_ref, middle_ref, third_ref, flag_ref, out_ref, lines_ref, wins_ref
):
    real = jnp.concatenate([x_ref[pl.ds(jj, 64, stride=8), :] for jj in range(4)], axis=0)
    imag = jnp.concatenate([x_ref[pl.ds(4 + jj, 64, stride=8), :] for jj in range(4)], axis=0)
    special = flag_ref[0] == 0
    lone = jnp.where(special, imag, real)
    kept = jnp.where(special, jnp.zeros_like(imag), imag)
    at, bt, ct, dt = turns_ref[0], turns_ref[1], turns_ref[2], turns_ref[3]
    stacked = jnp.concatenate(
        [
            jnp.concatenate([real * at - kept * bt, lone * ct - kept * dt], axis=1),
            jnp.concatenate([real * bt + kept * at, -(lone * dt + kept * ct)], axis=1),
        ],
        axis=0,
    )
    stage = jnp.dot(second_ref[...], stacked, precision=highest, preferred_element_type=f32)
    mid_real, mid_imag = middle_ref[0], middle_ref[1]
    for half in range(2):
        part = stage[:, half * 128 : half * 128 + 128]
        part_real, part_imag = part[:256], part[256:]
        turned = jnp.concatenate(
            [
                part_real * mid_real - part_imag * mid_imag,
                part_real * mid_imag + part_imag * mid_real,
            ],
            axis=1,
        )
        lines = lax.dot_general(
            third_ref[...],
            turned,
            (((1,), (1,)), ((), ())),
            precision=highest,
            preferred_element_type=f32,
        )
        c_at = lax.broadcasted_iota(jnp.int32, (72, 256), 0)
        q_at = lax.broadcasted_iota(jnp.int32, (72, 256), 1)
        outside = jnp.logical_and(q_at == 0, c_at == (0 if half else 64))
        for ri in range(2):
            arr = half * 2 + ri
            kept_lines = jnp.where(outside, 0.0, lines[ri * 72 : ri * 72 + 72])
            for tile in range(2):
                lines_ref[arr, tile] = kept_lines[:, tile * 128 : tile * 128 + 128]
    low = lax.broadcasted_iota(jnp.int32, (16, 128), 1) < 64

    def swap(tile):
        return pltpu.roll(tile, 64, 1)

    for arr in range(4):
        for u in range(2):
            wins_ref[arr, u] = lines_ref[arr, u]
            wins_ref[arr, 2, pl.ds(u, 32, stride=2), :] = lines_ref[arr, u, 0:32, :]
        wins_ref[arr, 2, 64:65, :] = lines_ref[arr, 0, 32:33, :]
        t = [
            [lines_ref[arr, w, pl.ds(v, 16, stride=3), :] for w in range(2)]
            for v in range(3)
        ]
        firsts = (
            t[0][0],
            jnp.where(low, swap(t[0][1]), swap(t[1][0])),
            t[1][1],
            jnp.where(low, swap(t[2][0]), swap(t[2][1])),
        )
        seconds = (t[0][1], swap(t[1][0]), t[2][0], swap(t[2][1]))
        s0 = lines_ref[arr, 0, 0:16, :]
        s1 = lines_ref[arr, 1, 0:16, :]
        quarters = (swap(s0), s0, swap(s1), s1)
        for w in range(4):
            wins_ref[arr, 3, pl.ds(w, 16, stride=4), :] = firsts[w]
            wins_ref[arr, 4, pl.ds(w, 16, stride=4), :] = jnp.where(low, seconds[w], quarters[w])
        wins_ref[arr, 3, 64:65, :] = lines_ref[arr, 0, 48:49, :]
        wins_ref[arr, 4, 64:65, :] = pltpu.roll(lines_ref[arr, 0, 16:17, :], 64, 1)
    lane = lax.broadcasted_iota(jnp.int32, (64, 128), 1)
    tails = jnp.zeros((64, 128), f32)
    for arr in range(4):
        for tile in range(5):
            row = arr * 5 + tile
            out_ref[pl.ds(row, 64, stride=ROWS_OUT), :] = wins_ref[arr, tile, 0:64, :]
        for g, (tile, column) in enumerate(((0, 0), (2, 0), (3, 0), (4, 64))):
            value = wins_ref[arr, tile, 1:65, column : column + 1]
            tails = jnp.where(lane == arr * 4 + g, value, tails)
    out_ref[pl.ds(20, 64, stride=ROWS_OUT), :] = tails


def taps_kernel(v_ref, flip_ref, high_ref, low_ref):
    natural = [
        pltpu.roll(
            jnp.broadcast_to(v_ref[part, 0], (256, 256)), 0, 1, stride=1, stride_axis=0
        )[:, :128]
        for part in range(2)
    ]
    for lower in range(2):
        pair = [-natural[1], natural[0]] if lower else natural
        splits = halves(jnp.concatenate(pair, axis=1))
        for target, split in zip((high_ref, low_ref), splits):
            for at in range(2):
                base = lower * 256 + at * 128
                target[0, base : base + 64] = jnp.dot(
                    flip_ref[...],
                    split[at * 128 : at * 128 + 64],
                    preferred_element_type=f32,
                ).astype(bf16)
                target[0, base + 64 : base + 128] = split[at * 128 + 64 : at * 128 + 128]


def power_kernel(
    rows_ref,
    x_ref,
    high_ref,
    low_ref,
    one_ref,
    two_ref,
    three_ref,
    out_ref,
    gathered_ref,
    win_high_ref,
    win_low_ref,
    sum_ref,
    lower_ref,
):
    step = pl.program_id(0)

    @pl.when(step == 0)
    def _():
        tails = x_ref[pl.ds(20, 64, stride=ROWS_OUT), :]
        tails = jnp.transpose(jnp.concatenate([tails, tails], axis=0))
        lane = lax.broadcasted_iota(jnp.int32, (1, 128), 1)
        for ri in range(2):
            for tile in range(5):
                block = jnp.concatenate(
                    [
                        x_ref[pl.ds((half * 2 + ri) * 5 + tile, 64, stride=ROWS_OUT), :]
                        for half in (1, 0)
                    ],
                    axis=0,
                )
                block = jnp.transpose(block)
                if tile < 2:
                    gathered_ref[ri, tile * 128 : tile * 128 + 128] = block
                elif tile == 2:
                    gathered_ref[ri, BASES[1] : BASES[1] + 128] = block
                elif tile == 3:
                    gathered_ref[ri, BASES[2] : BASES[2] + 128] = block
                else:
                    gathered_ref[ri, BASES[2] + 128 : BASES[2] + 192] = block[:64]
                    gathered_ref[ri, BASES[3] : BASES[3] + 64] = block[64:]
            for g in range(4):
                upper = tails[(2 + ri) * 4 + g : (2 + ri) * 4 + g + 1]
                lower = tails[ri * 4 + g : ri * 4 + g + 1]
                at = BASES[g] + COUNTS[g]
                gathered_ref[ri, at : at + 1] = jnp.where(lane < 64, upper, lower)
        places = [(beta * 64, beta, 4) for beta in range(4)]
        places += [(256 + v * 64, BASES[1] + v, 2) for v in range(2)]
        places += [(384 + v * 64, BASES[2] + v, 3) for v in range(3)]
        places += [(576, BASES[3], 1)]
        for target, source, stride in places:
            for ri in range(2):
                for shift in range(2):
                    at = source + shift
                    block = gathered_ref[ri, pl.ds(at, 64, stride=stride), :]
                    span = slice((ri * 2 + shift) * 128, (ri * 2 + shift) * 128 + 128)
                    high, low = halves(block)
                    win_high_ref[target : target + 64, span] = high
                    win_low_ref[target : target + 64, span] = low

    response = jnp.dot(win_high_ref[...], high_ref[0], preferred_element_type=f32)
    response += jnp.dot(win_low_ref[...], high_ref[0], preferred_element_type=f32)
    response += jnp.dot(win_high_ref[...], low_ref[0], preferred_element_type=f32)
    real, imag = response[:, :128], response[:, 128:]
    power = real * real + imag * imag
    sum_ref[pl.ds(step * 256, 256), :] = power[:256]
    high, low = halves(power[256:])
    lower_ref[step, :, 0:128] = high
    lower_ref[step, :, 128:256] = low

    @pl.when(step == TEMPL - 1)
    def _():
        for t in range(TEMPL):
            r1, r2, r3 = rows_ref[0, t], rows_ref[1, t], rows_ref[2, t]
            single = jnp.dot(lower_ref[r1, 320:384], one_ref[...], preferred_element_type=f32)
            double = jnp.dot(lower_ref[r2, 0:128], two_ref[...], preferred_element_type=f32)
            triple = [
                jnp.dot(
                    lower_ref[r3, 128 + 64 * v : 192 + 64 * v],
                    three_ref[v],
                    preferred_element_type=f32,
                )
                for v in range(3)
            ]
            thirds = (
                triple[0][:, :128],
                triple[0][:, 128:] + triple[1][:, :128],
                triple[1][:, 128:] + triple[2][:, :128],
                triple[2][:, 128:],
            )
            for beta in range(4):
                v, u = beta // 2, beta % 2
                at = t * 256 + beta * 64
                sum_ref[at : at + 64, :] = (
                    sum_ref[at : at + 64, :]
                    + single[:, beta * 128 : beta * 128 + 128]
                    + double[v * 64 : v * 64 + 64, u * 128 : u * 128 + 128]
                    + thirds[beta]
                )
        for beta in range(4):
            for i in range(64):
                b = 4 * i + beta
                for t in range(0, TEMPL, 8):
                    out_ref[t : t + 8, b * 128 : b * 128 + 128] = sum_ref[
                        pl.ds(t * 256 + beta * 64 + i, 8, stride=256), :
                    ]


def swap_blocks(values):
    return lax.all_to_all(values, "freq", split_axis=0, concat_axis=0, tiled=True)


def turn_tables(position):
    m = 128 * jnp.asarray(row_order(), jnp.int32)[:, None] + jnp.arange(128, dtype=jnp.int32)
    tables = []
    for residue in (position, jnp.where(position == 0, 64, position)):
        angles = (m * residue).astype(f32) * (-2.0 * math.pi / SAMPLES)
        tables += [jnp.cos(angles), jnp.sin(angles)]
    return jnp.stack(tables)


def tap_rows(kernels, half_widths):
    offsets = jnp.abs(jnp.arange(2 * MAXHALF + 1, dtype=jnp.int32) - MAXHALF)
    inside = offsets[None, :] <= half_widths[:, None]
    taps = jnp.where(inside[None], kernels, 0.0)
    return jnp.concatenate(
        [taps[:, :, 0:1], jnp.zeros((2, TEMPL, 127), f32), taps[:, :, :0:-1]], axis=2
    ).reshape(2, TEMPL, 1, 256)


def whole(shape):
    return pl.BlockSpec(shape, lambda i: (0,) * len(shape))


def on_device(series, kernels, half_widths, sub_rows):
    position = lax.axis_index("freq")
    blocks = series.reshape(2, MEMBERS, 4, LANES).transpose(1, 0, 2, 3).reshape(512, LANES)
    arrived = swap_blocks(blocks)
    streams = pl.pallas_call(
        first_kernel, out_shape=jax.ShapeDtypeStruct((512, LANES), f32), name="first"
    )(jnp.asarray(first_matrix()), arrived)
    arrived = swap_blocks(streams)
    outgoing = pl.pallas_call(
        spectrum_kernel,
        in_specs=[pl.BlockSpec()] * 5 + [pl.BlockSpec(memory_space=pltpu.SMEM)],
        out_shape=jax.ShapeDtypeStruct((MEMBERS * ROWS_OUT, LANES), f32),
        scratch_shapes=[pltpu.VMEM((4, 2, 72, 128), f32), pltpu.VMEM((4, 5, 72, 128), f32)],
        name="spectrum",
    )(
        arrived,
        turn_tables(position),
        jnp.asarray(second_matrix()),
        jnp.asarray(middle_twiddle()),
        jnp.asarray(third_matrix()),
        position.reshape(1),
    )
    arrived = swap_blocks(outgoing)
    matrix = jax.ShapeDtypeStruct((TEMPL, 512, 256), bf16)
    one_block = pl.BlockSpec((1, 512, 256), lambda i: (i, 0, 0))
    tap_high, tap_low = pl.pallas_call(
        taps_kernel,
        grid=(TEMPL,),
        in_specs=[pl.BlockSpec((2, 1, 1, 256), lambda i: (0, i, 0, 0)), whole((64, 64))],
        out_specs=[one_block, one_block],
        out_shape=[matrix, matrix],
        name="taps",
    )(tap_rows(kernels, half_widths), jnp.asarray(flip_matrix()))
    one, two, threes = (jnp.asarray(m) for m in spread_matrices())
    return pl.pallas_call(
        power_kernel,
        grid=(TEMPL,),
        in_specs=[
            pl.BlockSpec(memory_space=pltpu.SMEM),
            whole((MEMBERS * ROWS_OUT, LANES)),
            one_block,
            one_block,
            whole((256, 512)),
            whole((256, 256)),
            whole((3, 256, 256)),
        ],
        out_specs=whole((TEMPL, 256 * LANES)),
        out_shape=jax.ShapeDtypeStruct((TEMPL, 256 * LANES), f32),
        scratch_shapes=[
            pltpu.VMEM((2, GATHERED, 128), f32),
            pltpu.VMEM((WINDOWS, 512), bf16),
            pltpu.VMEM((WINDOWS, 512), bf16),
            pltpu.VMEM((TEMPL * 256, 128), f32),
            pltpu.VMEM((TEMPL, 384, 256), bf16),
        ],
        name="power",
    )(sub_rows, arrived, tap_high, tap_low, one, two, threes)


def solution(mesh):
    in_specs = (P(("dm", "freq")), P(), P(), P())
    out_specs = P(None, ("dm", "freq"))
    return jax.shard_map(
        on_device, mesh=mesh, in_specs=in_specs, out_specs=out_specs, check_vma=False
    )
```

```python
import math

import jax
import jax.numpy as jnp
import numpy as np
from jax import lax
from jax.experimental import pallas as pl
from jax.experimental.pallas import tpu as pltpu
from jax.sharding import PartitionSpec as P

SAMPLES = 4194304
TEMPL = 16
MAXHALF = 64
MEMBERS = 64
LANES = 128
ROWS_OUT = 24

f32 = jnp.float32
bf16 = jnp.bfloat16

MAIN, HALF2, HALF3, HALF1 = 0, 1, 2, 3
COUNTS = (256, 128, 192, 64)
BASES = (0, 264, 400, 600)
GATHERED = 672
WINDOWS = 640
PAIRS = 2
STEPS = TEMPL // 2 // PAIRS


def unit(product, length):
    angles = np.asarray(product, np.float64) % length * (-2.0 * math.pi / length)
    return np.cos(angles), np.sin(angles)


def first_matrix():
    matrix = np.zeros((128, 128))
    wide = np.arange(128)
    for k0 in range(64):
        real, imag = unit(k0 * wide, 128)
        matrix[2 * k0] = real
        matrix[2 * k0 + 1] = imag
    matrix[1] = unit(64 * wide, 128)[0]
    return matrix.astype(np.float32)


def row_order():
    at = np.arange(256)
    return 4 * (at % 64) + at // 64


def second_matrix():
    q, a = np.arange(256)[:, None], row_order()[None, :]
    real, imag = unit(q * a, 256)
    return np.block([[real, -imag], [imag, real]]).astype(np.float32)


def middle_twiddle():
    q, b = np.arange(256)[:, None], np.arange(128)[None, :]
    real, imag = unit(q * b, 32768)
    return np.stack([real, imag]).astype(np.float32)


def third_matrix():
    c, b = np.arange(72)[:, None], np.arange(128)[None, :]
    real, imag = unit(c * b, 128)
    norm = 1.0 / math.sqrt(SAMPLES)
    return (np.block([[real, -imag], [imag, real]]) * norm).astype(np.float32)


def spread_matrices():
    lane, s = np.arange(128)[:, None], np.arange(128)[None, :]
    pairs = []
    for pair in range(2):
        columns = []
        for u in range(2):
            beta = 2 * pair + u
            pieces = [lane == 32 * beta + s // 4, lane == 64 * u + s // 2]
            for v in (pair, pair + 1):
                pieces.append(128 * v + lane == 96 * beta + 3 * s // 4)
            columns.append(np.concatenate([np.concatenate([m, m]) for m in pieces]))
        pairs.append(np.concatenate(columns, axis=1))
    return np.stack(pairs).astype(bf16)


def flip_matrix():
    at = np.arange(64)
    return ((64 - at[:, None]) % 64 == at[None, :]).astype(bf16)


def halves(values):
    high = values.astype(bf16)
    return high, (values - high.astype(f32)).astype(bf16)


def constant_halves(matrix):
    high = matrix.astype(bf16)
    low = (matrix - high.astype(np.float32)).astype(bf16)
    return jnp.asarray(np.stack([high, low]))


def product(left, right, dims=((1,), (0,))):
    (left_at,), (right_at,) = dims
    return lax.dot_general(
        jnp.concatenate([left[0], left[0], left[1]], axis=left_at),
        jnp.concatenate([right[0], right[1], right[0]], axis=right_at),
        (dims, ((), ())),
        preferred_element_type=f32,
    )


def first_kernel(matrix_ref, x_ref, out_ref):
    samples = jnp.concatenate([x_ref[pl.ds(jj, 128, stride=4), :] for jj in range(4)], axis=1)
    streams = product((matrix_ref[0], matrix_ref[1]), halves(samples))
    for jj in range(4):
        out_ref[pl.ds(jj, 128, stride=4), :] = streams[:, jj * 128 : jj * 128 + 128]


def spectrum_kernel(
    x_ref, turns_ref, second_ref, middle_ref, third_ref, flag_ref, out_ref, lines_ref, wins_ref
):
    real = jnp.concatenate([x_ref[pl.ds(jj, 64, stride=8), :] for jj in range(4)], axis=0)
    imag = jnp.concatenate([x_ref[pl.ds(4 + jj, 64, stride=8), :] for jj in range(4)], axis=0)
    special = flag_ref[0] == 0
    lone = jnp.where(special, imag, real)
    kept = jnp.where(special, jnp.zeros_like(imag), imag)
    at, bt, ct, dt = turns_ref[0], turns_ref[1], turns_ref[2], turns_ref[3]
    stacked = jnp.concatenate(
        [
            jnp.concatenate([real * at - kept * bt, lone * ct - kept * dt], axis=1),
            jnp.concatenate([real * bt + kept * at, -(lone * dt + kept * ct)], axis=1),
        ],
        axis=0,
    )
    stage = product((second_ref[0], second_ref[1]), halves(stacked))
    mid_real, mid_imag = middle_ref[0], middle_ref[1]
    for half in range(2):
        part = stage[:, half * 128 : half * 128 + 128]
        part_real, part_imag = part[:256], part[256:]
        turned = jnp.concatenate(
            [
                part_real * mid_real - part_imag * mid_imag,
                part_real * mid_imag + part_imag * mid_real,
            ],
            axis=1,
        )
        lines = product((third_ref[0], third_ref[1]), halves(turned), ((1,), (1,)))
        c_at = lax.broadcasted_iota(jnp.int32, (72, 256), 0)
        q_at = lax.broadcasted_iota(jnp.int32, (72, 256), 1)
        outside = jnp.logical_and(q_at == 0, c_at == (0 if half else 64))
        for ri in range(2):
            arr = half * 2 + ri
            kept_lines = jnp.where(outside, 0.0, lines[ri * 72 : ri * 72 + 72])
            for tile in range(2):
                lines_ref[arr, tile] = kept_lines[:, tile * 128 : tile * 128 + 128]
    low = lax.broadcasted_iota(jnp.int32, (16, 128), 1) < 64

    def swap(tile):
        return pltpu.roll(tile, 64, 1)

    for arr in range(4):
        for u in range(2):
            wins_ref[arr, u] = lines_ref[arr, u]
            wins_ref[arr, 2, pl.ds(u, 32, stride=2), :] = lines_ref[arr, u, 0:32, :]
        wins_ref[arr, 2, 64:65, :] = lines_ref[arr, 0, 32:33, :]
        t = [
            [lines_ref[arr, w, pl.ds(v, 16, stride=3), :] for w in range(2)]
            for v in range(3)
        ]
        firsts = (
            t[0][0],
            jnp.where(low, swap(t[0][1]), swap(t[1][0])),
            t[1][1],
            jnp.where(low, swap(t[2][0]), swap(t[2][1])),
        )
        seconds = (t[0][1], swap(t[1][0]), t[2][0], swap(t[2][1]))
        s0 = lines_ref[arr, 0, 0:16, :]
        s1 = lines_ref[arr, 1, 0:16, :]
        quarters = (swap(s0), s0, swap(s1), s1)
        for w in range(4):
            wins_ref[arr, 3, pl.ds(w, 16, stride=4), :] = firsts[w]
            wins_ref[arr, 4, pl.ds(w, 16, stride=4), :] = jnp.where(low, seconds[w], quarters[w])
        wins_ref[arr, 3, 64:65, :] = lines_ref[arr, 0, 48:49, :]
        wins_ref[arr, 4, 64:65, :] = pltpu.roll(lines_ref[arr, 0, 16:17, :], 64, 1)
    lane = lax.broadcasted_iota(jnp.int32, (64, 128), 1)
    tails = jnp.zeros((64, 128), f32)
    for arr in range(4):
        for tile in range(5):
            row = arr * 5 + tile
            out_ref[pl.ds(row, 64, stride=ROWS_OUT), :] = wins_ref[arr, tile, 0:64, :]
        for g, (tile, column) in enumerate(((0, 0), (2, 0), (3, 0), (4, 64))):
            value = wins_ref[arr, tile, 1:65, column : column + 1]
            tails = jnp.where(lane == arr * 4 + g, value, tails)
    out_ref[pl.ds(20, 64, stride=ROWS_OUT), :] = tails


def taps_kernel(v_ref, flip_ref, high_ref, low_ref):
    natural = [
        jnp.concatenate(
            [
                pltpu.roll(
                    jnp.broadcast_to(v_ref[part, t], (256, 256)), 0, 1, stride=1, stride_axis=0
                )[:, :128]
                for t in range(2)
            ],
            axis=1,
        )
        for part in range(2)
    ]
    trio = (natural[0], natural[1] - natural[0], natural[0] + natural[1])
    for which, matrix in enumerate(trio):
        for target, split in zip((high_ref, low_ref), halves(matrix)):
            for base in (0, 128):
                target[0, which, base : base + 64] = jnp.dot(
                    flip_ref[...], split[base : base + 64], preferred_element_type=f32
                ).astype(bf16)
                target[0, which, base + 64 : base + 128] = split[base + 64 : base + 128]


def gather_windows(x_ref, gathered_ref, win_high_ref, win_low_ref):
    tails = x_ref[pl.ds(20, 64, stride=ROWS_OUT), :]
    tails = jnp.transpose(jnp.concatenate([tails, tails], axis=0))
    lane = lax.broadcasted_iota(jnp.int32, (1, 128), 1)
    for ri in range(2):
        for tile in range(5):
            block = jnp.concatenate(
                [
                    x_ref[pl.ds((half * 2 + ri) * 5 + tile, 64, stride=ROWS_OUT), :]
                    for half in (1, 0)
                ],
                axis=0,
            )
            block = jnp.transpose(block)
            if tile < 2:
                gathered_ref[ri, tile * 128 : tile * 128 + 128] = block
            elif tile == 2:
                gathered_ref[ri, BASES[1] : BASES[1] + 128] = block
            elif tile == 3:
                gathered_ref[ri, BASES[2] : BASES[2] + 128] = block
            else:
                gathered_ref[ri, BASES[2] + 128 : BASES[2] + 192] = block[:64]
                gathered_ref[ri, BASES[3] : BASES[3] + 64] = block[64:]
        for g in range(4):
            upper = tails[(2 + ri) * 4 + g : (2 + ri) * 4 + g + 1]
            lower = tails[ri * 4 + g : ri * 4 + g + 1]
            at = BASES[g] + COUNTS[g]
            gathered_ref[ri, at : at + 1] = jnp.where(lane < 64, upper, lower)
    places = [(beta * 64, beta, 4) for beta in range(4)]
    places += [(256 + v * 64, BASES[1] + v, 2) for v in range(2)]
    places += [(384 + v * 64, BASES[2] + v, 3) for v in range(3)]
    places += [(576, BASES[3], 1)]
    for target, source, stride in places:
        for shift in range(2):
            real, imag = (
                gathered_ref[ri, pl.ds(source + shift, 64, stride=stride), :] for ri in range(2)
            )
            span = slice(shift * 128, shift * 128 + 128)
            for which, values in enumerate((real + imag, real, imag)):
                high, low = halves(values)
                win_high_ref[which, target : target + 64, span] = high
                win_low_ref[which, target : target + 64, span] = low


def power_kernel(
    rows_ref,
    x_ref,
    high_ref,
    low_ref,
    spread_ref,
    out_ref,
    gathered_ref,
    win_high_ref,
    win_low_ref,
    sum_ref,
    lower_ref,
):
    step = pl.program_id(0)

    @pl.when(step == 0)
    def _():
        gather_windows(x_ref, gathered_ref, win_high_ref, win_low_ref)

    @pl.when(step < STEPS)
    def _():
        for pair in range(PAIRS):
            parts = [
                product(
                    (win_high_ref[which], win_low_ref[which]),
                    (high_ref[pair, which], low_ref[pair, which]),
                )
                for which in range(3)
            ]
            real = parts[0] - parts[2]
            imag = parts[0] + parts[1]
            power = real * real + imag * imag
            for at in range(2):
                t = (step * PAIRS + pair) * 2 + at
                span = slice(at * 128, at * 128 + 128)
                sum_ref[pl.ds(t * 256, 256), :] = power[:256, span]
                high, low = halves(power[256:, span])
                lower_ref[t, :, 0:128] = high
                lower_ref[t, :, 128:256] = low

    @pl.when(step >= STEPS)
    def _():
        first = (step - STEPS) * 8
        picks = [[rows_ref[h, first + t] for t in range(8)] for h in range(3)]

        def rows_of(h, at):
            return jnp.concatenate([lower_ref[r, at : at + 64] for r in picks[h]], axis=0)

        for pair in range(2):
            sources = (
                rows_of(0, 320),
                rows_of(1, 64 * pair),
                rows_of(2, 128 + 64 * pair),
                rows_of(2, 192 + 64 * pair),
            )
            spread = jnp.dot(
                jnp.concatenate(sources, axis=1), spread_ref[pair], preferred_element_type=f32
            )
            for u in range(2):
                beta = 2 * pair + u
                for t in range(8):
                    own = sum_ref[pl.ds((first + t) * 256 + beta * 64, 64), :]
                    out_ref[pl.ds(beta * 8 + t, 64, stride=32), :] = (
                        own + spread[t * 64 : t * 64 + 64, u * 128 : u * 128 + 128]
                    )


def swap_blocks(values):
    return lax.all_to_all(values, "freq", split_axis=0, concat_axis=0, tiled=True)


def turn_tables(position):
    m = 128 * jnp.asarray(row_order(), jnp.int32)[:, None] + jnp.arange(128, dtype=jnp.int32)
    tables = []
    for residue in (position, jnp.where(position == 0, 64, position)):
        angles = (m * residue).astype(f32) * (-2.0 * math.pi / SAMPLES)
        tables += [jnp.cos(angles), jnp.sin(angles)]
    return jnp.stack(tables)


def tap_rows(kernels, half_widths):
    offsets = jnp.abs(jnp.arange(2 * MAXHALF + 1, dtype=jnp.int32) - MAXHALF)
    inside = offsets[None, :] <= half_widths[:, None]
    taps = jnp.where(inside[None], kernels, 0.0)
    return jnp.concatenate(
        [taps[:, :, 0:1], jnp.zeros((2, TEMPL, 127), f32), taps[:, :, :0:-1]], axis=2
    ).reshape(2, TEMPL, 1, 256)


def whole(shape):
    return pl.BlockSpec(shape, lambda i: (0,) * len(shape))


def grant(mebibytes):
    return pltpu.CompilerParams(vmem_limit_bytes=mebibytes << 20)


def on_device(series, kernels, half_widths, sub_rows):
    position = lax.axis_index("freq")
    blocks = series.reshape(2, MEMBERS, 4, LANES).transpose(1, 0, 2, 3).reshape(512, LANES)
    arrived = swap_blocks(blocks)
    streams = pl.pallas_call(
        first_kernel,
        out_shape=jax.ShapeDtypeStruct((512, LANES), f32),
        compiler_params=grant(4),
        name="first",
    )(constant_halves(first_matrix()), arrived)
    arrived = swap_blocks(streams)
    outgoing = pl.pallas_call(
        spectrum_kernel,
        in_specs=[pl.BlockSpec()] * 5 + [pl.BlockSpec(memory_space=pltpu.SMEM)],
        out_shape=jax.ShapeDtypeStruct((MEMBERS * ROWS_OUT, LANES), f32),
        scratch_shapes=[pltpu.VMEM((4, 2, 72, 128), f32), pltpu.VMEM((4, 5, 72, 128), f32)],
        compiler_params=grant(12),
        name="spectrum",
    )(
        arrived,
        turn_tables(position),
        constant_halves(second_matrix()),
        jnp.asarray(middle_twiddle()),
        constant_halves(third_matrix()),
        position.reshape(1),
    )
    arrived = swap_blocks(outgoing)
    matrix = jax.ShapeDtypeStruct((TEMPL // 2, 3, 256, 256), bf16)
    tap_block = pl.BlockSpec((1, 3, 256, 256), lambda i: (i, 0, 0, 0))
    tap_high, tap_low = pl.pallas_call(
        taps_kernel,
        grid=(TEMPL // 2,),
        in_specs=[pl.BlockSpec((2, 2, 1, 256), lambda i: (0, i, 0, 0)), whole((64, 64))],
        out_specs=[tap_block, tap_block],
        out_shape=[matrix, matrix],
        compiler_params=grant(58),
        name="taps",
    )(tap_rows(kernels, half_widths), jnp.asarray(flip_matrix()))
    tap_block = pl.BlockSpec(
        (PAIRS, 3, 256, 256), lambda i: (jnp.minimum(i, STEPS - 1), 0, 0, 0)
    )
    summed = pl.pallas_call(
        power_kernel,
        grid=(STEPS + 2,),
        in_specs=[
            pl.BlockSpec(memory_space=pltpu.SMEM),
            whole((MEMBERS * ROWS_OUT, LANES)),
            tap_block,
            tap_block,
            whole((2, 1024, 256)),
        ],
        out_specs=pl.BlockSpec((2048, LANES), lambda i: (jnp.maximum(i - STEPS, 0), 0)),
        out_shape=jax.ShapeDtypeStruct((TEMPL * 256, LANES), f32),
        scratch_shapes=[
            pltpu.VMEM((2, GATHERED, 128), f32),
            pltpu.VMEM((3, WINDOWS, 256), bf16),
            pltpu.VMEM((3, WINDOWS, 256), bf16),
            pltpu.VMEM((TEMPL * 256, 128), f32),
            pltpu.VMEM((TEMPL, 384, 256), bf16),
        ],
        compiler_params=grant(50),
        name="power",
    )(sub_rows, arrived, tap_high, tap_low, jnp.asarray(spread_matrices()))
    return summed.reshape(2, 256, 8, LANES).transpose(0, 2, 1, 3).reshape(TEMPL, 256 * LANES)


def solution(mesh):
    in_specs = (P(("dm", "freq")), P(), P(), P())
    out_specs = P(None, ("dm", "freq"))
    return jax.shard_map(
        on_device, mesh=mesh, in_specs=in_specs, out_specs=out_specs, check_vma=False
    )
```

```python
import math

import jax
import jax.numpy as jnp
import numpy as np
from jax import lax
from jax.experimental import pallas as pl
from jax.experimental.pallas import tpu as pltpu
from jax.sharding import PartitionSpec as P

SAMPLES = 4194304
TEMPL = 16
MAXHALF = 64
MEMBERS = 64
LANES = 128
ROWS_OUT = 21

f32 = jnp.float32
bf16 = jnp.bfloat16

MAIN, HALF2, HALF3, HALF1 = 0, 1, 2, 3
COUNTS = (256, 128, 192, 64)
BASES = (0, 264, 400, 600)
GATHERED = 672
WINDOWS = 640
QUAD = 4
QUADS = TEMPL // QUAD


def unit(product, length):
    angles = np.asarray(product, np.float64) % length * (-2.0 * math.pi / length)
    return np.cos(angles), np.sin(angles)


def first_matrix():
    matrix = np.zeros((128, 128))
    wide = np.arange(128)
    for k0 in range(64):
        real, imag = unit(k0 * wide, 128)
        matrix[2 * k0] = real
        matrix[2 * k0 + 1] = imag
    matrix[1] = unit(64 * wide, 128)[0]
    return matrix.astype(np.float32)


def row_order():
    at = np.arange(256)
    return 4 * (at % 64) + at // 64


def second_matrix():
    q, a = np.arange(256)[:, None], row_order()[None, :]
    real, imag = unit(q * a, 256)
    return np.block([[real, -imag], [imag, real]]).astype(np.float32)


def middle_twiddle():
    q, b = np.arange(256)[:, None], np.arange(128)[None, :]
    real, imag = unit(q * b, 32768)
    return np.stack([real, imag]).astype(np.float32)


def third_matrix():
    c, b = np.arange(72)[:, None], np.arange(128)[None, :]
    real, imag = unit(c * b, 128)
    norm = 1.0 / math.sqrt(SAMPLES)
    return (np.block([[real, -imag], [imag, real]]) * norm).astype(np.float32)


def spread_matrices():
    lane, s = np.arange(128)[:, None], np.arange(128)[None, :]
    pairs = []
    for pair in range(2):
        columns = []
        for u in range(2):
            beta = 2 * pair + u
            pieces = [lane == 32 * beta + s // 4, lane == 64 * u + s // 2]
            for v in (pair, pair + 1):
                pieces.append(128 * v + lane == 96 * beta + 3 * s // 4)
            columns.append(np.concatenate(pieces))
        pairs.append(np.concatenate(columns, axis=1))
    return np.stack(pairs).astype(bf16)


def flip_matrix():
    at = np.arange(64)
    return ((64 - at[:, None]) % 64 == at[None, :]).astype(bf16)


def halves(values):
    high = values.astype(bf16)
    return high, (values - high.astype(f32)).astype(bf16)


def constant_halves(matrix):
    high = matrix.astype(bf16)
    low = (matrix - high.astype(np.float32)).astype(bf16)
    return jnp.asarray(np.stack([high, low]))


def product(left, right, dims=((1,), (0,))):
    (left_at,), (right_at,) = dims
    return lax.dot_general(
        jnp.concatenate([left[0], left[0], left[1]], axis=left_at),
        jnp.concatenate([right[0], right[1], right[0]], axis=right_at),
        (dims, ((), ())),
        preferred_element_type=f32,
    )


def pack_kernel(series_hbm, out_hbm, held_ref, fetched, stored):
    parts = [(h, pl.ds(16 * at, 16), 4 * h + at) for at in range(4) for h in range(2)]
    fetches = [
        pltpu.make_async_copy(series_hbm.at[h, span], held_ref.at[h, span], fetched.at[slot])
        for h, span, slot in parts
    ]
    stores = [
        pltpu.make_async_copy(held_ref.at[h, span], out_hbm.at[span, h], stored.at[slot])
        for h, span, slot in parts
    ]
    for fetch in fetches:
        fetch.start()
    for fetch, store in zip(fetches, stores):
        fetch.wait()
        store.start()
    for store in stores:
        store.wait()


def tables_kernel(*refs):
    count = len(refs) // 2
    for source, target in zip(refs[:count], refs[count:]):
        target[...] = source[...]


def first_kernel(matrix_ref, x_ref, out_ref):
    samples = jnp.concatenate([x_ref[pl.ds(jj, 128, stride=4), :] for jj in range(4)], axis=1)
    streams = product((matrix_ref[0], matrix_ref[1]), halves(samples))
    for jj in range(4):
        out_ref[pl.ds(jj, 128, stride=4), :] = streams[:, jj * 128 : jj * 128 + 128]


def spectrum_kernel(
    x_ref, turns_ref, second_ref, middle_ref, third_ref, flag_ref, out_ref, lines_ref, wins_ref
):
    real = jnp.concatenate([x_ref[pl.ds(jj, 64, stride=8), :] for jj in range(4)], axis=0)
    imag = jnp.concatenate([x_ref[pl.ds(4 + jj, 64, stride=8), :] for jj in range(4)], axis=0)
    special = flag_ref[0] == 0
    lone = jnp.where(special, imag, real)
    kept = jnp.where(special, jnp.zeros_like(imag), imag)
    at, bt, ct, dt = turns_ref[0], turns_ref[1], turns_ref[2], turns_ref[3]
    stacked = jnp.concatenate(
        [
            jnp.concatenate([real * at - kept * bt, lone * ct - kept * dt], axis=1),
            jnp.concatenate([real * bt + kept * at, -(lone * dt + kept * ct)], axis=1),
        ],
        axis=0,
    )
    stage = product((second_ref[0], second_ref[1]), halves(stacked))
    mid_real, mid_imag = middle_ref[0], middle_ref[1]
    for half in range(2):
        part = stage[:, half * 128 : half * 128 + 128]
        part_real, part_imag = part[:256], part[256:]
        turned = jnp.concatenate(
            [
                part_real * mid_real - part_imag * mid_imag,
                part_real * mid_imag + part_imag * mid_real,
            ],
            axis=1,
        )
        lines = product((third_ref[0], third_ref[1]), halves(turned), ((1,), (1,)))
        c_at = lax.broadcasted_iota(jnp.int32, (72, 256), 0)
        q_at = lax.broadcasted_iota(jnp.int32, (72, 256), 1)
        outside = jnp.logical_and(q_at == 0, c_at == (0 if half else 64))
        for ri in range(2):
            arr = half * 2 + ri
            kept_lines = jnp.where(outside, 0.0, lines[ri * 72 : ri * 72 + 72])
            for tile in range(2):
                lines_ref[arr, tile] = kept_lines[:, tile * 128 : tile * 128 + 128]
    low = lax.broadcasted_iota(jnp.int32, (16, 128), 1) < 64

    def swap(tile):
        return pltpu.roll(tile, 64, 1)

    for arr in range(4):
        for u in range(2):
            wins_ref[arr, u] = lines_ref[arr, u]
            wins_ref[arr, 2, pl.ds(u, 32, stride=2), :] = lines_ref[arr, u, 0:32, :]
        wins_ref[arr, 2, 64:65, :] = lines_ref[arr, 0, 32:33, :]
        t = [
            [lines_ref[arr, w, pl.ds(v, 16, stride=3), :] for w in range(2)]
            for v in range(3)
        ]
        firsts = (
            t[0][0],
            jnp.where(low, swap(t[0][1]), swap(t[1][0])),
            t[1][1],
            jnp.where(low, swap(t[2][0]), swap(t[2][1])),
        )
        seconds = (t[0][1], swap(t[1][0]), t[2][0], swap(t[2][1]))
        s0 = lines_ref[arr, 0, 0:16, :]
        s1 = lines_ref[arr, 1, 0:16, :]
        quarters = (swap(s0), s0, swap(s1), s1)
        for w in range(4):
            wins_ref[arr, 3, pl.ds(w, 16, stride=4), :] = firsts[w]
            wins_ref[arr, 4, pl.ds(w, 16, stride=4), :] = jnp.where(low, seconds[w], quarters[w])
        wins_ref[arr, 3, 64:65, :] = lines_ref[arr, 0, 48:49, :]
        wins_ref[arr, 4, 64:65, :] = pltpu.roll(lines_ref[arr, 0, 16:17, :], 64, 1)
    lane = lax.broadcasted_iota(jnp.int32, (64, 128), 1)
    tails = jnp.zeros((64, 128), f32)
    for arr in range(4):
        for tile in range(5):
            row = arr * 5 + tile
            out_ref[pl.ds(row, 64, stride=ROWS_OUT), :] = wins_ref[arr, tile, 0:64, :]
        for g, (tile, column) in enumerate(((0, 0), (2, 0), (3, 0), (4, 64))):
            value = wins_ref[arr, tile, 1:65, column : column + 1]
            tails = jnp.where(lane == arr * 4 + g, value, tails)
    out_ref[pl.ds(20, 64, stride=ROWS_OUT), :] = tails


def taps_kernel(v_ref, flip_ref, taps_ref):
    natural = [
        jnp.concatenate(
            [
                pltpu.roll(
                    jnp.broadcast_to(v_ref[part, t], (256, 256)), 0, 1, stride=1, stride_axis=0
                )[:, :128]
                for t in range(QUAD)
            ],
            axis=1,
        )
        for part in range(2)
    ]
    trio = (natural[0], natural[1] - natural[0], natural[0] + natural[1])
    for which, matrix in enumerate(trio):
        for level, split in enumerate(halves(matrix)):
            for base in (0, 128):
                taps_ref[0, level, which, base : base + 64] = jnp.dot(
                    flip_ref[...], split[base : base + 64], preferred_element_type=f32
                ).astype(bf16)
                taps_ref[0, level, which, base + 64 : base + 128] = split[
                    base + 64 : base + 128
                ]


def gather_windows(x_ref, gathered_ref, win_high_ref, win_low_ref):
    tails = x_ref[pl.ds(20, 64, stride=ROWS_OUT), :]
    tails = jnp.transpose(jnp.concatenate([tails, tails], axis=0))
    lane = lax.broadcasted_iota(jnp.int32, (1, 128), 1)
    for ri in range(2):
        for tile in range(5):
            block = jnp.concatenate(
                [
                    x_ref[pl.ds((half * 2 + ri) * 5 + tile, 64, stride=ROWS_OUT), :]
                    for half in (1, 0)
                ],
                axis=0,
            )
            block = jnp.transpose(block)
            if tile < 2:
                gathered_ref[ri, tile * 128 : tile * 128 + 128] = block
            elif tile == 2:
                gathered_ref[ri, BASES[1] : BASES[1] + 128] = block
            elif tile == 3:
                gathered_ref[ri, BASES[2] : BASES[2] + 128] = block
            else:
                gathered_ref[ri, BASES[2] + 128 : BASES[2] + 192] = block[:64]
                gathered_ref[ri, BASES[3] : BASES[3] + 64] = block[64:]
        for g in range(4):
            upper = tails[(2 + ri) * 4 + g : (2 + ri) * 4 + g + 1]
            lower = tails[ri * 4 + g : ri * 4 + g + 1]
            at = BASES[g] + COUNTS[g]
            gathered_ref[ri, at : at + 1] = jnp.where(lane < 64, upper, lower)
    places = [(beta * 64, beta, 4) for beta in range(4)]
    places += [(256 + v * 64, BASES[1] + v, 2) for v in range(2)]
    places += [(384 + v * 64, BASES[2] + v, 3) for v in range(3)]
    places += [(576, BASES[3], 1)]
    for target, source, stride in places:
        for shift in range(2):
            real, imag = (
                gathered_ref[ri, pl.ds(source + shift, 64, stride=stride), :] for ri in range(2)
            )
            span = slice(shift * 128, shift * 128 + 128)
            for which, values in enumerate((real + imag, real, imag)):
                high, low = halves(values)
                win_high_ref[which, target : target + 64, span] = high
                win_low_ref[which, target : target + 64, span] = low


def power_kernel(
    rows_ref,
    x_ref,
    taps_hbm,
    spread_ref,
    out_hbm,
    gathered_ref,
    win_high_ref,
    win_low_ref,
    taps_ref,
    parts_ref,
    squares_ref,
    sum_ref,
    lower_ref,
    out_ref,
    fetched,
    stored,
):
    fetches = [
        pltpu.make_async_copy(taps_hbm.at[quad], taps_ref.at[quad], fetched.at[quad])
        for quad in range(QUADS)
    ]
    for fetch in fetches:
        fetch.start()
    gather_windows(x_ref, gathered_ref, win_high_ref, win_low_ref)

    for quad in range(QUADS):
        if quad < 2:
            for fetch in fetches[1:] if quad else fetches[:1]:
                fetch.wait()

        def part(which):
            return product(
                (win_high_ref[which], win_low_ref[which]),
                (taps_ref[quad, 0, which], taps_ref[quad, 1, which]),
            )

        slot = quad % 2
        parts_ref[slot] = part(0)
        imag = parts_ref[slot] + part(1)
        squares_ref[slot] = imag * imag
        real = parts_ref[slot] - part(2)
        power = real * real + squares_ref[slot]
        for at in range(QUAD):
            t = quad * QUAD + at
            span = slice(at * 128, at * 128 + 128)
            sum_ref[t] = power[:256, span]
            lower_ref[t] = power[256:, span]

    stores = []
    for chunk in range(2):
        first = chunk * 8
        places = ((0, 320), (1, 0), (1, 64), (2, 128), (2, 192), (2, 256))
        sources = [
            jnp.concatenate(
                halves(
                    jnp.concatenate(
                        [lower_ref[rows_ref[h, first + t], at : at + 64] for t in range(8)], axis=0
                    )
                ),
                axis=1,
            )
            for h, at in places
        ]
        for pair in range(2):
            spread = jnp.dot(
                jnp.concatenate(
                    [sources[0], sources[1 + pair], sources[3 + pair], sources[4 + pair]], axis=1
                ),
                jnp.concatenate(
                    [spread_ref[pair, 128 * (k // 2) : 128 * (k // 2) + 128] for k in range(8)],
                    axis=0,
                ),
                preferred_element_type=f32,
            )
            for u in range(2):
                beta = 2 * pair + u
                for t in range(8):
                    out_ref[chunk, beta, pl.ds(t, 64, stride=8), :] = (
                        sum_ref[first + t, beta * 64 : beta * 64 + 64]
                        + spread[t * 64 : t * 64 + 64, u * 128 : u * 128 + 128]
                    )
                store = pltpu.make_async_copy(
                    out_ref.at[chunk, beta].reshape(64, 8, 128), out_hbm.at[chunk, :, beta], stored.at[chunk, beta]
                )
                store.start()
                stores.append(store)
    for store in stores:
        store.wait()


def swap_blocks(values):
    return lax.all_to_all(values, "freq", split_axis=0, concat_axis=0, tiled=True)


def turn_tables(position):
    m = 128 * jnp.asarray(row_order(), jnp.int32)[:, None] + jnp.arange(128, dtype=jnp.int32)
    tables = []
    for residue in (position, jnp.where(position == 0, 64, position)):
        angles = (m * residue).astype(f32) * (-2.0 * math.pi / SAMPLES)
        tables += [jnp.cos(angles), jnp.sin(angles)]
    return jnp.stack(tables)


def tap_rows(kernels, half_widths):
    offsets = jnp.abs(jnp.arange(2 * MAXHALF + 1, dtype=jnp.int32) - MAXHALF)
    inside = offsets[None, :] <= half_widths[:, None]
    taps = jnp.where(inside[None], kernels, 0.0)
    return jnp.concatenate(
        [taps[:, :, 0:1], jnp.zeros((2, TEMPL, 127), f32), taps[:, :, :0:-1]], axis=2
    ).reshape(2, TEMPL, 1, 256)


def whole(shape):
    return pl.BlockSpec(shape, lambda i: (0,) * len(shape))


def grant(mebibytes):
    return pltpu.CompilerParams(
        vmem_limit_bytes=mebibytes << 20
    )


def on_device(series, kernels, half_widths, sub_rows):
    position = lax.axis_index("freq")
    blocks = pl.pallas_call(
        pack_kernel,
        in_specs=[pl.BlockSpec(memory_space=pltpu.HBM)],
        out_specs=pl.BlockSpec(memory_space=pltpu.HBM),
        out_shape=jax.ShapeDtypeStruct((MEMBERS, 2, 4, LANES), f32),
        scratch_shapes=[
            pltpu.VMEM((2, MEMBERS, 4, LANES), f32),
            pltpu.SemaphoreType.DMA((8,)),
            pltpu.SemaphoreType.DMA((8,)),
        ],
        name="pack",
    )(series.reshape(2, MEMBERS, 4, LANES))
    arrived = swap_blocks(blocks).reshape(512, LANES)
    tables = (
        constant_halves(first_matrix()),
        constant_halves(second_matrix()),
        jnp.asarray(middle_twiddle()),
        constant_halves(third_matrix()),
    )
    first, second, middle, third = pl.pallas_call(
        tables_kernel,
        out_shape=[jax.ShapeDtypeStruct(table.shape, table.dtype) for table in tables],
        compiler_params=grant(12),
        name="tables",
    )(*tables)
    streams = pl.pallas_call(
        first_kernel,
        in_specs=[pl.BlockSpec(memory_space=pltpu.VMEM)] * 2,
        out_shape=jax.ShapeDtypeStruct((512, LANES), f32),
        compiler_params=grant(4),
        name="first",
    )(first, arrived)
    arrived = swap_blocks(streams)
    outgoing = pl.pallas_call(
        spectrum_kernel,
        in_specs=[pl.BlockSpec(memory_space=pltpu.VMEM)] * 5 + [pl.BlockSpec(memory_space=pltpu.SMEM)],
        out_shape=jax.ShapeDtypeStruct((MEMBERS * ROWS_OUT, LANES), f32),
        scratch_shapes=[pltpu.VMEM((4, 2, 72, 128), f32), pltpu.VMEM((4, 5, 72, 128), f32)],
        compiler_params=grant(12),
        name="spectrum",
    )(
        arrived,
        turn_tables(position),
        second,
        middle,
        third,
        position.reshape(1),
    )
    outgoing = outgoing.reshape(MEMBERS, ROWS_OUT, 1, LANES)
    arrived = swap_blocks(outgoing).reshape(MEMBERS * ROWS_OUT, LANES)
    taps_shape = (2, 3, 256, 128 * QUAD)
    taps = pl.pallas_call(
        taps_kernel,
        grid=(QUADS,),
        in_specs=[pl.BlockSpec((2, QUAD, 1, 256), lambda i: (0, i, 0, 0)), whole((64, 64))],
        out_specs=pl.BlockSpec((1, *taps_shape), lambda i: (i, 0, 0, 0, 0)),
        out_shape=jax.ShapeDtypeStruct((QUADS, *taps_shape), bf16),
        compiler_params=grant(58),
        name="taps",
    )(tap_rows(kernels, half_widths), jnp.asarray(flip_matrix()))
    summed = pl.pallas_call(
        power_kernel,
        in_specs=[
            pl.BlockSpec(memory_space=pltpu.SMEM),
            pl.BlockSpec(memory_space=pltpu.VMEM),
            pl.BlockSpec(memory_space=pltpu.HBM),
            pl.BlockSpec(memory_space=pltpu.VMEM),
        ],
        out_specs=pl.BlockSpec(memory_space=pltpu.HBM),
        out_shape=jax.ShapeDtypeStruct((2, 64, 4, 8, LANES), f32),
        scratch_shapes=[
            pltpu.VMEM((2, GATHERED, 128), f32),
            pltpu.VMEM((3, WINDOWS, 256), bf16),
            pltpu.VMEM((3, WINDOWS, 256), bf16),
            pltpu.VMEM((QUADS, *taps_shape), bf16),
            pltpu.VMEM((2, WINDOWS, 128 * QUAD), f32),
            pltpu.VMEM((2, WINDOWS, 128 * QUAD), f32),
            pltpu.VMEM((TEMPL, 256, 128), f32),
            pltpu.VMEM((TEMPL, 384, 128), f32),
            pltpu.VMEM((2, 4, 512, 128), f32),
            pltpu.SemaphoreType.DMA((QUADS,)),
            pltpu.SemaphoreType.DMA((2, 4)),
        ],
        compiler_params=grant(50),
        name="power",
    )(sub_rows, arrived, taps, jnp.asarray(spread_matrices()))
    return summed.reshape(2, 256, 8, LANES).transpose(0, 2, 1, 3).reshape(TEMPL, 256 * LANES)


def solution(mesh):
    in_specs = (P(("dm", "freq")), P(), P(), P())
    out_specs = P(None, ("dm", "freq"))
    return jax.shard_map(
        on_device, mesh=mesh, in_specs=in_specs, out_specs=out_specs, check_vma=False
    )
```

```python
import math

import jax
import jax.numpy as jnp
import numpy as np
from jax import lax
from jax.experimental import pallas as pl
from jax.experimental.pallas import tpu as pltpu
from jax.sharding import PartitionSpec as P

SAMPLES = 4194304
TEMPL = 16
MAXHALF = 64
MEMBERS = 64
LANES = 128
ROWS_OUT = 21

f32 = jnp.float32
bf16 = jnp.bfloat16

MAIN, HALF2, HALF3, HALF1 = 0, 1, 2, 3
COUNTS = (256, 128, 192, 64)
BASES = (0, 264, 400, 600)
GATHERED = 672
WINDOWS = 640
QUAD = 4
QUADS = TEMPL // QUAD


def unit(product, length):
    angles = np.asarray(product, np.float64) % length * (-2.0 * math.pi / length)
    return np.cos(angles), np.sin(angles)


def first_matrix():
    matrix = np.zeros((128, 128))
    wide = np.arange(128)
    for k0 in range(64):
        real, imag = unit(k0 * wide, 128)
        matrix[2 * k0] = real
        matrix[2 * k0 + 1] = imag
    matrix[1] = unit(64 * wide, 128)[0]
    return matrix.astype(np.float32)


def row_order():
    at = np.arange(256)
    return 4 * (at % 64) + at // 64


def second_matrix():
    q, a = np.arange(256)[:, None], row_order()[None, :]
    real, imag = unit(q * a, 256)
    return np.block([[real, -imag], [imag, real]]).astype(np.float32)


def middle_twiddle():
    q, b = np.arange(256)[:, None], np.arange(128)[None, :]
    real, imag = unit(q * b, 32768)
    return np.stack([real, imag]).astype(np.float32)


def third_matrix():
    c, b = np.arange(72)[:, None], np.arange(128)[None, :]
    real, imag = unit(c * b, 128)
    norm = 1.0 / math.sqrt(SAMPLES)
    return (np.block([[real, -imag], [imag, real]]) * norm).astype(np.float32)


def spread_matrices():
    lane, s = np.arange(128)[:, None], np.arange(128)[None, :]
    pairs = []
    for pair in range(2):
        columns = []
        for u in range(2):
            beta = 2 * pair + u
            pieces = [lane == 32 * beta + s // 4, lane == 64 * u + s // 2]
            for v in (pair, pair + 1):
                pieces.append(128 * v + lane == 96 * beta + 3 * s // 4)
            columns.append(np.concatenate(pieces))
        pairs.append(np.concatenate(columns, axis=1))
    return np.stack(pairs).astype(bf16)


def flip_matrix():
    at = np.arange(64)
    return ((64 - at[:, None]) % 64 == at[None, :]).astype(bf16)


def halves(values):
    high = values.astype(bf16)
    return high, (values - high.astype(f32)).astype(bf16)


def constant_halves(matrix):
    high = matrix.astype(bf16)
    low = (matrix - high.astype(np.float32)).astype(bf16)
    return jnp.asarray(np.stack([high, low]))


def product(left, right, dims=((1,), (0,))):
    (left_at,), (right_at,) = dims
    return lax.dot_general(
        jnp.concatenate([left[0], left[0], left[1]], axis=left_at),
        jnp.concatenate([right[0], right[1], right[0]], axis=right_at),
        (dims, ((), ())),
        preferred_element_type=f32,
    )


def pack_kernel(series_hbm, out_hbm, held_ref, fetched, stored):
    parts = [(h, pl.ds(16 * at, 16), 4 * h + at) for at in range(4) for h in range(2)]
    fetches = [
        pltpu.make_async_copy(series_hbm.at[h, span], held_ref.at[h, span], fetched.at[slot])
        for h, span, slot in parts
    ]
    stores = [
        pltpu.make_async_copy(held_ref.at[h, span], out_hbm.at[span, h], stored.at[slot])
        for h, span, slot in parts
    ]
    for fetch in fetches:
        fetch.start()
    for fetch, store in zip(fetches, stores):
        fetch.wait()
        store.start()
    for store in stores:
        store.wait()


def tables_kernel(*refs):
    count = len(refs) // 2
    for source, target in zip(refs[:count], refs[count:]):
        target[...] = source[...]


def first_kernel(matrix_ref, x_ref, out_ref):
    samples = jnp.concatenate([x_ref[pl.ds(jj, 128, stride=4), :] for jj in range(4)], axis=1)
    streams = product((matrix_ref[0], matrix_ref[1]), halves(samples))
    for jj in range(4):
        out_ref[pl.ds(jj, 128, stride=4), :] = streams[:, jj * 128 : jj * 128 + 128]


def spectrum_kernel(
    x_ref, turns_ref, second_ref, middle_ref, third_ref, flag_ref, out_ref, lines_ref, wins_ref
):
    real = jnp.concatenate([x_ref[pl.ds(jj, 64, stride=8), :] for jj in range(4)], axis=0)
    imag = jnp.concatenate([x_ref[pl.ds(4 + jj, 64, stride=8), :] for jj in range(4)], axis=0)
    special = flag_ref[0] == 0
    lone = jnp.where(special, imag, real)
    kept = jnp.where(special, jnp.zeros_like(imag), imag)
    at, bt, ct, dt = turns_ref[0], turns_ref[1], turns_ref[2], turns_ref[3]
    stacked = jnp.concatenate(
        [
            jnp.concatenate([real * at - kept * bt, lone * ct - kept * dt], axis=1),
            jnp.concatenate([real * bt + kept * at, -(lone * dt + kept * ct)], axis=1),
        ],
        axis=0,
    )
    stage = product((second_ref[0], second_ref[1]), halves(stacked))
    mid_real, mid_imag = middle_ref[0], middle_ref[1]
    for half in range(2):
        part = stage[:, half * 128 : half * 128 + 128]
        part_real, part_imag = part[:256], part[256:]
        turned = jnp.concatenate(
            [
                part_real * mid_real - part_imag * mid_imag,
                part_real * mid_imag + part_imag * mid_real,
            ],
            axis=1,
        )
        lines = product((third_ref[0], third_ref[1]), halves(turned), ((1,), (1,)))
        c_at = lax.broadcasted_iota(jnp.int32, (72, 256), 0)
        q_at = lax.broadcasted_iota(jnp.int32, (72, 256), 1)
        outside = jnp.logical_and(q_at == 0, c_at == (0 if half else 64))
        for ri in range(2):
            arr = half * 2 + ri
            kept_lines = jnp.where(outside, 0.0, lines[ri * 72 : ri * 72 + 72])
            for tile in range(2):
                lines_ref[arr, tile] = kept_lines[:, tile * 128 : tile * 128 + 128]
    low = lax.broadcasted_iota(jnp.int32, (16, 128), 1) < 64

    def swap(tile):
        return pltpu.roll(tile, 64, 1)

    for arr in range(4):
        for u in range(2):
            wins_ref[arr, u] = lines_ref[arr, u]
            wins_ref[arr, 2, pl.ds(u, 32, stride=2), :] = lines_ref[arr, u, 0:32, :]
        wins_ref[arr, 2, 64:65, :] = lines_ref[arr, 0, 32:33, :]
        t = [
            [lines_ref[arr, w, pl.ds(v, 16, stride=3), :] for w in range(2)]
            for v in range(3)
        ]
        firsts = (
            t[0][0],
            jnp.where(low, swap(t[0][1]), swap(t[1][0])),
            t[1][1],
            jnp.where(low, swap(t[2][0]), swap(t[2][1])),
        )
        seconds = (t[0][1], swap(t[1][0]), t[2][0], swap(t[2][1]))
        s0 = lines_ref[arr, 0, 0:16, :]
        s1 = lines_ref[arr, 1, 0:16, :]
        quarters = (swap(s0), s0, swap(s1), s1)
        for w in range(4):
            wins_ref[arr, 3, pl.ds(w, 16, stride=4), :] = firsts[w]
            wins_ref[arr, 4, pl.ds(w, 16, stride=4), :] = jnp.where(low, seconds[w], quarters[w])
        wins_ref[arr, 3, 64:65, :] = lines_ref[arr, 0, 48:49, :]
        wins_ref[arr, 4, 64:65, :] = pltpu.roll(lines_ref[arr, 0, 16:17, :], 64, 1)
    lane = lax.broadcasted_iota(jnp.int32, (64, 128), 1)
    tails = jnp.zeros((64, 128), f32)
    for arr in range(4):
        for tile in range(5):
            row = arr * 5 + tile
            out_ref[pl.ds(row, 64, stride=ROWS_OUT), :] = wins_ref[arr, tile, 0:64, :]
        for g, (tile, column) in enumerate(((0, 0), (2, 0), (3, 0), (4, 64))):
            value = wins_ref[arr, tile, 1:65, column : column + 1]
            tails = jnp.where(lane == arr * 4 + g, value, tails)
    out_ref[pl.ds(20, 64, stride=ROWS_OUT), :] = tails


def taps_kernel(v_ref, flip_ref, taps_ref):
    natural = [
        jnp.concatenate(
            [
                pltpu.roll(
                    jnp.broadcast_to(v_ref[part, t], (256, 256)), 0, 1, stride=1, stride_axis=0
                )[:, :128]
                for t in range(QUAD)
            ],
            axis=1,
        )
        for part in range(2)
    ]
    trio = (natural[0] + natural[1], natural[0], natural[1])
    for which, matrix in enumerate(trio):
        for level, split in enumerate(halves(matrix)):
            for base in (0, 128):
                taps_ref[0, level, which, base : base + 64] = jnp.dot(
                    flip_ref[...], split[base : base + 64], preferred_element_type=f32
                ).astype(bf16)
                taps_ref[0, level, which, base + 64 : base + 128] = split[
                    base + 64 : base + 128
                ]


def gather(x_ref, gathered_ref, tails, ri):
    lane = lax.broadcasted_iota(jnp.int32, (1, 128), 1)
    for tile in range(5):
        block = jnp.concatenate(
            [
                x_ref[pl.ds((half * 2 + ri) * 5 + tile, 64, stride=ROWS_OUT), :]
                for half in (1, 0)
            ],
            axis=0,
        )
        block = jnp.transpose(block)
        if tile < 2:
            gathered_ref[ri, tile * 128 : tile * 128 + 128] = block
        elif tile == 2:
            gathered_ref[ri, BASES[1] : BASES[1] + 128] = block
        elif tile == 3:
            gathered_ref[ri, BASES[2] : BASES[2] + 128] = block
        else:
            gathered_ref[ri, BASES[2] + 128 : BASES[2] + 192] = block[:64]
            gathered_ref[ri, BASES[3] : BASES[3] + 64] = block[64:]
    for g in range(4):
        upper = tails[(2 + ri) * 4 + g : (2 + ri) * 4 + g + 1]
        lower = tails[ri * 4 + g : ri * 4 + g + 1]
        at = BASES[g] + COUNTS[g]
        gathered_ref[ri, at : at + 1] = jnp.where(lane < 64, upper, lower)


def make_windows(gathered_ref, win_high_ref, win_low_ref, which):
    places = [(beta * 64, beta, 4) for beta in range(4)]
    places += [(256 + v * 64, BASES[1] + v, 2) for v in range(2)]
    places += [(384 + v * 64, BASES[2] + v, 3) for v in range(3)]
    places += [(576, BASES[3], 1)]
    for target, source, stride in places:
        for shift in range(2):
            values = gathered_ref[0, pl.ds(source + shift, 64, stride=stride), :]
            if which:
                imag = gathered_ref[1, pl.ds(source + shift, 64, stride=stride), :]
                values = imag - values if which == 1 else imag + values
            span = slice(shift * 128, shift * 128 + 128)
            high, low = halves(values)
            win_high_ref[which, target : target + 64, span] = high
            win_low_ref[which, target : target + 64, span] = low


def power_kernel(
    rows_ref,
    x_ref,
    head_ref,
    rest_hbm,
    spread_ref,
    out_hbm,
    gathered_ref,
    win_high_ref,
    win_low_ref,
    rest_ref,
    parts_ref,
    squares_ref,
    sum_ref,
    lower_ref,
    out_ref,
    fetched,
    stored,
):
    fetches = [
        pltpu.make_async_copy(rest_hbm.at[at], rest_ref.at[at], fetched.at[at])
        for at in range(QUADS - 1)
    ]
    for fetch in fetches:
        fetch.start()
    tails = x_ref[pl.ds(20, 64, stride=ROWS_OUT), :]
    tails = jnp.transpose(jnp.concatenate([tails, tails], axis=0))
    gather(x_ref, gathered_ref, tails, 0)
    make_windows(gathered_ref, win_high_ref, win_low_ref, 0)

    for quad in range(QUADS):
        taps_ref, at_quad = (rest_ref, quad - 1) if quad else (head_ref, 0)

        def part(which):
            return product(
                (win_high_ref[which], win_low_ref[which]),
                (taps_ref[at_quad, 0, which], taps_ref[at_quad, 1, which]),
            )

        slot = quad % 2
        parts_ref[slot] = part(0)
        if quad == 0:
            gather(x_ref, gathered_ref, tails, 1)
            make_windows(gathered_ref, win_high_ref, win_low_ref, 1)
            make_windows(gathered_ref, win_high_ref, win_low_ref, 2)
        imag = parts_ref[slot] + part(1)
        squares_ref[slot] = imag * imag
        if quad == 0:
            for fetch in fetches:
                fetch.wait()
        real = parts_ref[slot] - part(2)
        power = real * real + squares_ref[slot]
        for at in range(QUAD):
            t = quad * QUAD + at
            span = slice(at * 128, at * 128 + 128)
            sum_ref[t] = power[:256, span]
            lower_ref[t] = power[256:, span]

    stores = []
    for chunk in range(2):
        first = chunk * 8
        places = ((0, 320), (1, 0), (1, 64), (2, 128), (2, 192), (2, 256))
        sources = [
            jnp.concatenate(
                halves(
                    jnp.concatenate(
                        [lower_ref[rows_ref[h, first + t], at : at + 64] for t in range(8)], axis=0
                    )
                ),
                axis=1,
            )
            for h, at in places
        ]
        for pair in range(2):
            spread = jnp.dot(
                jnp.concatenate(
                    [sources[0], sources[1 + pair], sources[3 + pair], sources[4 + pair]], axis=1
                ),
                jnp.concatenate(
                    [spread_ref[pair, 128 * (k // 2) : 128 * (k // 2) + 128] for k in range(8)],
                    axis=0,
                ),
                preferred_element_type=f32,
            )
            for u in range(2):
                beta = 2 * pair + u
                for t in range(8):
                    out_ref[chunk, beta, pl.ds(t, 64, stride=8), :] = (
                        sum_ref[first + t, beta * 64 : beta * 64 + 64]
                        + spread[t * 64 : t * 64 + 64, u * 128 : u * 128 + 128]
                    )
                store = pltpu.make_async_copy(
                    out_ref.at[chunk, beta].reshape(64, 8, 128), out_hbm.at[chunk, :, beta], stored.at[chunk, beta]
                )
                store.start()
                stores.append(store)
    for store in stores:
        store.wait()


def swap_blocks(values):
    return lax.all_to_all(values, "freq", split_axis=0, concat_axis=0, tiled=True)


def turn_tables(position):
    m = 128 * jnp.asarray(row_order(), jnp.int32)[:, None] + jnp.arange(128, dtype=jnp.int32)
    tables = []
    for residue in (position, jnp.where(position == 0, 64, position)):
        angles = (m * residue).astype(f32) * (-2.0 * math.pi / SAMPLES)
        tables += [jnp.cos(angles), jnp.sin(angles)]
    return jnp.stack(tables)


def tap_rows(kernels, half_widths):
    offsets = jnp.abs(jnp.arange(2 * MAXHALF + 1, dtype=jnp.int32) - MAXHALF)
    inside = offsets[None, :] <= half_widths[:, None]
    taps = jnp.where(inside[None], kernels, 0.0)
    return jnp.concatenate(
        [taps[:, :, 0:1], jnp.zeros((2, TEMPL, 127), f32), taps[:, :, :0:-1]], axis=2
    ).reshape(2, TEMPL, 1, 256)


def whole(shape):
    return pl.BlockSpec(shape, lambda i: (0,) * len(shape))


def grant(mebibytes):
    return pltpu.CompilerParams(
        vmem_limit_bytes=mebibytes << 20
    )


def on_device(series, kernels, half_widths, sub_rows):
    position = lax.axis_index("freq")
    blocks = pl.pallas_call(
        pack_kernel,
        in_specs=[pl.BlockSpec(memory_space=pltpu.HBM)],
        out_specs=pl.BlockSpec(memory_space=pltpu.HBM),
        out_shape=jax.ShapeDtypeStruct((MEMBERS, 2, 4, LANES), f32),
        scratch_shapes=[
            pltpu.VMEM((2, MEMBERS, 4, LANES), f32),
            pltpu.SemaphoreType.DMA((8,)),
            pltpu.SemaphoreType.DMA((8,)),
        ],
        name="pack",
    )(series.reshape(2, MEMBERS, 4, LANES))
    arrived = swap_blocks(blocks).reshape(512, LANES)
    tables = (
        constant_halves(first_matrix()),
        constant_halves(second_matrix()),
        jnp.asarray(middle_twiddle()),
        constant_halves(third_matrix()),
    )
    first, second, middle, third = pl.pallas_call(
        tables_kernel,
        out_shape=[jax.ShapeDtypeStruct(table.shape, table.dtype) for table in tables],
        compiler_params=grant(12),
        name="tables",
    )(*tables)
    streams = pl.pallas_call(
        first_kernel,
        in_specs=[pl.BlockSpec(memory_space=pltpu.VMEM)] * 2,
        out_shape=jax.ShapeDtypeStruct((512, LANES), f32),
        compiler_params=grant(4),
        name="first",
    )(first, arrived)
    arrived = swap_blocks(streams)
    outgoing = pl.pallas_call(
        spectrum_kernel,
        in_specs=[pl.BlockSpec(memory_space=pltpu.VMEM)] * 5 + [pl.BlockSpec(memory_space=pltpu.SMEM)],
        out_shape=jax.ShapeDtypeStruct((MEMBERS * ROWS_OUT, LANES), f32),
        scratch_shapes=[pltpu.VMEM((4, 2, 72, 128), f32), pltpu.VMEM((4, 5, 72, 128), f32)],
        compiler_params=grant(12),
        name="spectrum",
    )(
        arrived,
        turn_tables(position),
        second,
        middle,
        third,
        position.reshape(1),
    )
    outgoing = outgoing.reshape(MEMBERS, ROWS_OUT, 1, LANES)
    arrived = swap_blocks(outgoing).reshape(MEMBERS * ROWS_OUT, LANES)
    taps_shape = (2, 3, 256, 128 * QUAD)
    rows = tap_rows(kernels, half_widths)
    flip = jnp.asarray(flip_matrix())

    def taps(start, count, mebibytes):
        return pl.pallas_call(
            taps_kernel,
            grid=(count,),
            in_specs=[
                pl.BlockSpec((2, QUAD, 1, 256), lambda i: (0, i + start, 0, 0)),
                whole((64, 64)),
            ],
            out_specs=pl.BlockSpec((1, *taps_shape), lambda i: (i, 0, 0, 0, 0)),
            out_shape=jax.ShapeDtypeStruct((count, *taps_shape), bf16),
            compiler_params=grant(mebibytes),
            name="taps",
        )(rows, flip)

    head, rest = taps(0, 1, 10), taps(1, QUADS - 1, 58)
    summed = pl.pallas_call(
        power_kernel,
        in_specs=[
            pl.BlockSpec(memory_space=pltpu.SMEM),
            pl.BlockSpec(memory_space=pltpu.VMEM),
            pl.BlockSpec(memory_space=pltpu.VMEM),
            pl.BlockSpec(memory_space=pltpu.HBM),
            pl.BlockSpec(memory_space=pltpu.VMEM),
        ],
        out_specs=pl.BlockSpec(memory_space=pltpu.HBM),
        out_shape=jax.ShapeDtypeStruct((2, 64, 4, 8, LANES), f32),
        scratch_shapes=[
            pltpu.VMEM((2, GATHERED, 128), f32),
            pltpu.VMEM((3, WINDOWS, 256), bf16),
            pltpu.VMEM((3, WINDOWS, 256), bf16),
            pltpu.VMEM((QUADS - 1, *taps_shape), bf16),
            pltpu.VMEM((2, WINDOWS, 128 * QUAD), f32),
            pltpu.VMEM((2, WINDOWS, 128 * QUAD), f32),
            pltpu.VMEM((TEMPL, 256, 128), f32),
            pltpu.VMEM((TEMPL, 384, 128), f32),
            pltpu.VMEM((2, 4, 512, 128), f32),
            pltpu.SemaphoreType.DMA((QUADS - 1,)),
            pltpu.SemaphoreType.DMA((2, 4)),
        ],
        compiler_params=grant(50),
        name="power",
    )(sub_rows, arrived, head, rest, jnp.asarray(spread_matrices()))
    return summed.reshape(2, 256, 8, LANES).transpose(0, 2, 1, 3).reshape(TEMPL, 256 * LANES)


def solution(mesh):
    in_specs = (P(("dm", "freq")), P(), P(), P())
    out_specs = P(None, ("dm", "freq"))
    return jax.shard_map(
        on_device, mesh=mesh, in_specs=in_specs, out_specs=out_specs, check_vma=False
    )
```

```python
import math

import jax
import jax.numpy as jnp
import numpy as np
from jax import lax
from jax.experimental import pallas as pl
from jax.experimental.pallas import tpu as pltpu
from jax.sharding import PartitionSpec as P

SAMPLES = 4194304
TEMPL = 16
MAXHALF = 64
MEMBERS = 64
LANES = 128
ROWS_OUT = 21

f32 = jnp.float32
bf16 = jnp.bfloat16

MAIN, HALF2, HALF3, HALF1 = 0, 1, 2, 3
COUNTS = (256, 128, 192, 64)
BASES = (0, 264, 400, 600)
GATHERED = 672
WINDOWS = 640
QUAD = 4
QUADS = TEMPL // QUAD


def unit(product, length):
    angles = np.asarray(product, np.float64) % length * (-2.0 * math.pi / length)
    return np.cos(angles), np.sin(angles)


def first_matrix():
    matrix = np.zeros((128, 128))
    wide = np.arange(128)
    for k0 in range(64):
        real, imag = unit(k0 * wide, 128)
        matrix[2 * k0] = real
        matrix[2 * k0 + 1] = imag
    matrix[1] = unit(64 * wide, 128)[0]
    return matrix.astype(np.float32)


def row_order():
    at = np.arange(256)
    return 4 * (at % 64) + at // 64


def second_matrix():
    q, a = np.arange(256)[:, None], row_order()[None, :]
    real, imag = unit(q * a, 256)
    return np.block([[real, -imag], [imag, real]]).astype(np.float32)


def middle_twiddle():
    q, b = np.arange(256)[:, None], np.arange(128)[None, :]
    real, imag = unit(q * b, 32768)
    return np.stack([real, imag]).astype(np.float32)


def third_matrix():
    c, b = np.arange(72)[:, None], np.arange(128)[None, :]
    real, imag = unit(c * b, 128)
    norm = 1.0 / math.sqrt(SAMPLES)
    return (np.block([[real, -imag], [imag, real]]) * norm).astype(np.float32)


def spread_matrices():
    lane, s = np.arange(128)[:, None], np.arange(128)[None, :]
    pairs = []
    for pair in range(2):
        columns = []
        for u in range(2):
            beta = 2 * pair + u
            pieces = [lane == 64 * u + s // 2]
            for v in (pair, pair + 1):
                pieces.append(128 * v + lane == 96 * beta + 3 * s // 4)
            columns.append(np.concatenate(pieces))
        pairs.append(np.concatenate(columns, axis=1))
    return np.stack(pairs).astype(bf16)


def flip_matrix():
    at = np.arange(64)
    return ((64 - at[:, None]) % 64 == at[None, :]).astype(bf16)


def halves(values):
    high = values.astype(bf16)
    return high, (values - high.astype(f32)).astype(bf16)


def constant_halves(matrix):
    high = matrix.astype(bf16)
    low = (matrix - high.astype(np.float32)).astype(bf16)
    return jnp.asarray(np.stack([high, low]))


def product(left, right, dims=((1,), (0,))):
    (left_at,), (right_at,) = dims
    return lax.dot_general(
        jnp.concatenate([left[0], left[0], left[1]], axis=left_at),
        jnp.concatenate([right[0], right[1], right[0]], axis=right_at),
        (dims, ((), ())),
        preferred_element_type=f32,
    )


def pack_kernel(series_hbm, out_hbm, held_ref, fetched, stored):
    parts = [(h, pl.ds(16 * at, 16), 4 * h + at) for at in range(4) for h in range(2)]
    fetches = [
        pltpu.make_async_copy(series_hbm.at[h, span], held_ref.at[h, span], fetched.at[slot])
        for h, span, slot in parts
    ]
    stores = [
        pltpu.make_async_copy(held_ref.at[h, span], out_hbm.at[span, h], stored.at[slot])
        for h, span, slot in parts
    ]
    for fetch in fetches:
        fetch.start()
    for fetch, store in zip(fetches, stores):
        fetch.wait()
        store.start()
    for store in stores:
        store.wait()


def tables_kernel(*refs):
    count = len(refs) // 2
    for source, target in zip(refs[:count], refs[count:]):
        target[...] = source[...]


def first_kernel(matrix_ref, x_ref, out_ref):
    samples = jnp.concatenate([x_ref[pl.ds(jj, 128, stride=4), :] for jj in range(4)], axis=1)
    streams = product((matrix_ref[0], matrix_ref[1]), halves(samples))
    for jj in range(4):
        out_ref[pl.ds(jj, 128, stride=4), :] = streams[:, jj * 128 : jj * 128 + 128]


def spectrum_kernel(
    x_ref, turns_ref, second_ref, middle_ref, third_ref, flag_ref, out_ref, lines_ref, wins_ref
):
    real = jnp.concatenate([x_ref[pl.ds(jj, 64, stride=8), :] for jj in range(4)], axis=0)
    imag = jnp.concatenate([x_ref[pl.ds(4 + jj, 64, stride=8), :] for jj in range(4)], axis=0)
    special = flag_ref[0] == 0
    lone = jnp.where(special, imag, real)
    kept = jnp.where(special, jnp.zeros_like(imag), imag)
    at, bt, ct, dt = turns_ref[0], turns_ref[1], turns_ref[2], turns_ref[3]
    stacked = jnp.concatenate(
        [
            jnp.concatenate([real * at - kept * bt, lone * ct - kept * dt], axis=1),
            jnp.concatenate([real * bt + kept * at, -(lone * dt + kept * ct)], axis=1),
        ],
        axis=0,
    )
    stage = product((second_ref[0], second_ref[1]), halves(stacked))
    mid_real, mid_imag = middle_ref[0], middle_ref[1]
    for half in range(2):
        part = stage[:, half * 128 : half * 128 + 128]
        part_real, part_imag = part[:256], part[256:]
        turned = jnp.concatenate(
            [
                part_real * mid_real - part_imag * mid_imag,
                part_real * mid_imag + part_imag * mid_real,
            ],
            axis=1,
        )
        lines = product((third_ref[0], third_ref[1]), halves(turned), ((1,), (1,)))
        c_at = lax.broadcasted_iota(jnp.int32, (72, 256), 0)
        q_at = lax.broadcasted_iota(jnp.int32, (72, 256), 1)
        outside = jnp.logical_and(q_at == 0, c_at == (0 if half else 64))
        for ri in range(2):
            arr = half * 2 + ri
            kept_lines = jnp.where(outside, 0.0, lines[ri * 72 : ri * 72 + 72])
            for tile in range(2):
                lines_ref[arr, tile] = kept_lines[:, tile * 128 : tile * 128 + 128]
    low = lax.broadcasted_iota(jnp.int32, (16, 128), 1) < 64

    def swap(tile):
        return pltpu.roll(tile, 64, 1)

    for arr in range(4):
        for u in range(2):
            wins_ref[arr, u] = lines_ref[arr, u]
            wins_ref[arr, 2, pl.ds(u, 32, stride=2), :] = lines_ref[arr, u, 0:32, :]
        wins_ref[arr, 2, 64:65, :] = lines_ref[arr, 0, 32:33, :]
        t = [
            [lines_ref[arr, w, pl.ds(v, 16, stride=3), :] for w in range(2)]
            for v in range(3)
        ]
        firsts = (
            t[0][0],
            jnp.where(low, swap(t[0][1]), swap(t[1][0])),
            t[1][1],
            jnp.where(low, swap(t[2][0]), swap(t[2][1])),
        )
        seconds = (t[0][1], swap(t[1][0]), t[2][0], swap(t[2][1]))
        s0 = lines_ref[arr, 0, 0:16, :]
        s1 = lines_ref[arr, 1, 0:16, :]
        quarters = (swap(s0), s0, swap(s1), s1)
        for w in range(4):
            wins_ref[arr, 3, pl.ds(w, 16, stride=4), :] = firsts[w]
            wins_ref[arr, 4, pl.ds(w, 16, stride=4), :] = jnp.where(low, seconds[w], quarters[w])
        wins_ref[arr, 3, 64:65, :] = lines_ref[arr, 0, 48:49, :]
        wins_ref[arr, 4, 64:65, :] = pltpu.roll(lines_ref[arr, 0, 16:17, :], 64, 1)
    lane = lax.broadcasted_iota(jnp.int32, (64, 128), 1)
    tails = jnp.zeros((64, 128), f32)
    for arr in range(4):
        for tile in range(5):
            row = arr * 5 + tile
            out_ref[pl.ds(row, 64, stride=ROWS_OUT), :] = wins_ref[arr, tile, 0:64, :]
        for g, (tile, column) in enumerate(((0, 0), (2, 0), (3, 0), (4, 64))):
            value = wins_ref[arr, tile, 1:65, column : column + 1]
            tails = jnp.where(lane == arr * 4 + g, value, tails)
    out_ref[pl.ds(20, 64, stride=ROWS_OUT), :] = tails


def taps_kernel(v_ref, flip_ref, taps_ref):
    natural = [
        jnp.concatenate(
            [
                pltpu.roll(
                    jnp.broadcast_to(v_ref[part, t], (256, 256)), 0, 1, stride=1, stride_axis=0
                )[:, :128]
                for t in range(QUAD)
            ],
            axis=1,
        )
        for part in range(2)
    ]
    trio = (natural[0] + natural[1], natural[0], natural[1])
    for which, matrix in enumerate(trio):
        for level, split in enumerate(halves(matrix)):
            for base in (0, 128):
                taps_ref[0, level, which, base : base + 64] = jnp.dot(
                    flip_ref[...], split[base : base + 64], preferred_element_type=f32
                ).astype(bf16)
                taps_ref[0, level, which, base + 64 : base + 128] = split[
                    base + 64 : base + 128
                ]


def gather(x_ref, gathered_ref, tails, ri):
    lane = lax.broadcasted_iota(jnp.int32, (1, 128), 1)
    for tile in range(5):
        block = jnp.concatenate(
            [
                x_ref[pl.ds((half * 2 + ri) * 5 + tile, 64, stride=ROWS_OUT), :]
                for half in (1, 0)
            ],
            axis=0,
        )
        block = jnp.transpose(block)
        if tile < 2:
            gathered_ref[ri, tile * 128 : tile * 128 + 128] = block
        elif tile == 2:
            gathered_ref[ri, BASES[1] : BASES[1] + 128] = block
        elif tile == 3:
            gathered_ref[ri, BASES[2] : BASES[2] + 128] = block
        else:
            gathered_ref[ri, BASES[2] + 128 : BASES[2] + 192] = block[:64]
            gathered_ref[ri, BASES[3] : BASES[3] + 64] = block[64:]
    for g in range(4):
        upper = tails[(2 + ri) * 4 + g : (2 + ri) * 4 + g + 1]
        lower = tails[ri * 4 + g : ri * 4 + g + 1]
        at = BASES[g] + COUNTS[g]
        gathered_ref[ri, at : at + 1] = jnp.where(lane < 64, upper, lower)


def make_windows(gathered_ref, win_high_ref, win_low_ref, which):
    places = [(beta * 64, beta, 4) for beta in range(4)]
    places += [(256 + v * 64, BASES[1] + v, 2) for v in range(2)]
    places += [(384 + v * 64, BASES[2] + v, 3) for v in range(3)]
    places += [(576, BASES[3], 1)]
    for target, source, stride in places:
        for shift in range(2):
            values = gathered_ref[0, pl.ds(source + shift, 64, stride=stride), :]
            if which:
                imag = gathered_ref[1, pl.ds(source + shift, 64, stride=stride), :]
                values = imag - values if which == 1 else imag + values
            span = slice(shift * 128, shift * 128 + 128)
            high, low = halves(values)
            win_high_ref[which, target : target + 64, span] = high
            win_low_ref[which, target : target + 64, span] = low


def power_kernel(
    rows_ref,
    x_ref,
    head_ref,
    rest_hbm,
    spread_ref,
    out_hbm,
    gathered_ref,
    win_high_ref,
    win_low_ref,
    rest_ref,
    parts_ref,
    squares_ref,
    sum_ref,
    lower_ref,
    out_ref,
    fetched,
    stored,
):
    fetches = [
        pltpu.make_async_copy(rest_hbm.at[at], rest_ref.at[at], fetched.at[at])
        for at in range(QUADS - 1)
    ]
    for fetch in fetches:
        fetch.start()
    tails = x_ref[pl.ds(20, 64, stride=ROWS_OUT), :]
    tails = jnp.transpose(jnp.concatenate([tails, tails], axis=0))
    gather(x_ref, gathered_ref, tails, 0)
    make_windows(gathered_ref, win_high_ref, win_low_ref, 0)

    for quad in range(QUADS):
        taps_ref, at_quad = (rest_ref, quad - 1) if quad else (head_ref, 0)

        def part(which):
            return product(
                (win_high_ref[which], win_low_ref[which]),
                (taps_ref[at_quad, 0, which], taps_ref[at_quad, 1, which]),
            )

        slot = quad % 2
        parts_ref[slot] = part(0)
        if quad == 0:
            gather(x_ref, gathered_ref, tails, 1)
            make_windows(gathered_ref, win_high_ref, win_low_ref, 1)
            make_windows(gathered_ref, win_high_ref, win_low_ref, 2)
        imag = parts_ref[slot] + part(1)
        squares_ref[slot] = imag * imag
        if quad == 0:
            for fetch in fetches:
                fetch.wait()
        real = parts_ref[slot] - part(2)
        power = real * real + squares_ref[slot]
        for at in range(QUAD):
            t = quad * QUAD + at
            span = slice(at * 128, at * 128 + 128)
            sum_ref[t] = power[:256, span]
            lower_ref[t] = power[256:, span]

    lane = lax.broadcasted_iota(jnp.int32, (64, 128), 1)
    def store(chunk, beta):
        return pltpu.make_async_copy(
            out_ref.at[chunk, beta].reshape(64, 8, 128),
            out_hbm.at[chunk, :, beta],
            stored.at[chunk, beta],
        )

    places = ((1, 0), (1, 64), (2, 128), (2, 192), (2, 256))
    for chunk in range(2):
        for begin in (chunk * 8, chunk * 8 + 4):
            sources = [
                jnp.concatenate(
                    halves(
                        jnp.concatenate(
                            [
                                lower_ref[rows_ref[h, begin + t], at : at + 64]
                                for t in range(4)
                            ],
                            axis=0,
                        )
                    ),
                    axis=1,
                )
                for h, at in places
            ]
            for pair in range(2):
                spread = jnp.dot(
                    jnp.concatenate([sources[pair], sources[2 + pair], sources[3 + pair]], axis=1),
                    jnp.concatenate(
                        [spread_ref[pair, 128 * (k // 2) : 128 * (k // 2) + 128] for k in range(6)],
                        axis=0,
                    ),
                    preferred_element_type=f32,
                )
                for u in range(2):
                    beta = 2 * pair + u
                    for t in range(4):
                        singles = jnp.take_along_axis(
                            lower_ref[rows_ref[0, begin + t], 320:384],
                            32 * beta + lane // 4,
                            axis=1,
                            mode="promise_in_bounds",
                        )
                        out_ref[chunk, beta, pl.ds((begin + t) % 8, 64, stride=8), :] = (
                            sum_ref[begin + t, beta * 64 : beta * 64 + 64]
                            + singles
                            + spread[t * 64 : t * 64 + 64, u * 128 : u * 128 + 128]
                        )
            if begin == 8:
                for beta in range(4):
                    store(0, beta).start()
    for beta in range(4):
        store(1, beta).start()
    for chunk in range(2):
        for beta in range(4):
            store(chunk, beta).wait()


def swap_blocks(values):
    return lax.all_to_all(values, "freq", split_axis=0, concat_axis=0, tiled=True)


def turn_tables(position):
    m = 128 * jnp.asarray(row_order(), jnp.int32)[:, None] + jnp.arange(128, dtype=jnp.int32)
    tables = []
    for residue in (position, jnp.where(position == 0, 64, position)):
        angles = (m * residue).astype(f32) * (-2.0 * math.pi / SAMPLES)
        tables += [jnp.cos(angles), jnp.sin(angles)]
    return jnp.stack(tables)


def tap_rows(kernels, half_widths):
    offsets = jnp.abs(jnp.arange(2 * MAXHALF + 1, dtype=jnp.int32) - MAXHALF)
    inside = offsets[None, :] <= half_widths[:, None]
    taps = jnp.where(inside[None], kernels, 0.0)
    return jnp.concatenate(
        [taps[:, :, 0:1], jnp.zeros((2, TEMPL, 127), f32), taps[:, :, :0:-1]], axis=2
    ).reshape(2, TEMPL, 1, 256)


def whole(shape):
    return pl.BlockSpec(shape, lambda i: (0,) * len(shape))


def grant(mebibytes):
    return pltpu.CompilerParams(
        vmem_limit_bytes=mebibytes << 20
    )


def on_device(series, kernels, half_widths, sub_rows):
    position = lax.axis_index("freq")
    blocks = pl.pallas_call(
        pack_kernel,
        in_specs=[pl.BlockSpec(memory_space=pltpu.HBM)],
        out_specs=pl.BlockSpec(memory_space=pltpu.HBM),
        out_shape=jax.ShapeDtypeStruct((MEMBERS, 2, 4, LANES), f32),
        scratch_shapes=[
            pltpu.VMEM((2, MEMBERS, 4, LANES), f32),
            pltpu.SemaphoreType.DMA((8,)),
            pltpu.SemaphoreType.DMA((8,)),
        ],
        name="pack",
    )(series.reshape(2, MEMBERS, 4, LANES))
    arrived = swap_blocks(blocks).reshape(512, LANES)
    tables = (
        constant_halves(first_matrix()),
        constant_halves(second_matrix()),
        jnp.asarray(middle_twiddle()),
        constant_halves(third_matrix()),
    )
    first, second, middle, third = pl.pallas_call(
        tables_kernel,
        out_shape=[jax.ShapeDtypeStruct(table.shape, table.dtype) for table in tables],
        compiler_params=grant(12),
        name="tables",
    )(*tables)
    streams = pl.pallas_call(
        first_kernel,
        in_specs=[pl.BlockSpec(memory_space=pltpu.VMEM)] * 2,
        out_shape=jax.ShapeDtypeStruct((512, LANES), f32),
        compiler_params=grant(4),
        name="first",
    )(first, arrived)
    arrived = swap_blocks(streams)
    outgoing = pl.pallas_call(
        spectrum_kernel,
        in_specs=[pl.BlockSpec(memory_space=pltpu.VMEM)] * 5 + [pl.BlockSpec(memory_space=pltpu.SMEM)],
        out_shape=jax.ShapeDtypeStruct((MEMBERS * ROWS_OUT, LANES), f32),
        scratch_shapes=[pltpu.VMEM((4, 2, 72, 128), f32), pltpu.VMEM((4, 5, 72, 128), f32)],
        compiler_params=grant(12),
        name="spectrum",
    )(
        arrived,
        turn_tables(position),
        second,
        middle,
        third,
        position.reshape(1),
    )
    outgoing = outgoing.reshape(MEMBERS, ROWS_OUT, 1, LANES)
    arrived = swap_blocks(outgoing).reshape(MEMBERS * ROWS_OUT, LANES)
    taps_shape = (2, 3, 256, 128 * QUAD)
    rows = tap_rows(kernels, half_widths)
    flip = jnp.asarray(flip_matrix())

    def taps(start, count, mebibytes):
        return pl.pallas_call(
            taps_kernel,
            grid=(count,),
            in_specs=[
                pl.BlockSpec((2, QUAD, 1, 256), lambda i: (0, i + start, 0, 0)),
                whole((64, 64)),
            ],
            out_specs=pl.BlockSpec((1, *taps_shape), lambda i: (i, 0, 0, 0, 0)),
            out_shape=jax.ShapeDtypeStruct((count, *taps_shape), bf16),
            compiler_params=grant(mebibytes),
            name="taps",
        )(rows, flip)

    head, rest = taps(0, 1, 10), taps(1, QUADS - 1, 58)
    summed = pl.pallas_call(
        power_kernel,
        in_specs=[
            pl.BlockSpec(memory_space=pltpu.SMEM),
            pl.BlockSpec(memory_space=pltpu.VMEM),
            pl.BlockSpec(memory_space=pltpu.VMEM),
            pl.BlockSpec(memory_space=pltpu.HBM),
            pl.BlockSpec(memory_space=pltpu.VMEM),
        ],
        out_specs=pl.BlockSpec(memory_space=pltpu.HBM),
        out_shape=jax.ShapeDtypeStruct((2, 64, 4, 8, LANES), f32),
        scratch_shapes=[
            pltpu.VMEM((2, GATHERED, 128), f32),
            pltpu.VMEM((3, WINDOWS, 256), bf16),
            pltpu.VMEM((3, WINDOWS, 256), bf16),
            pltpu.VMEM((QUADS - 1, *taps_shape), bf16),
            pltpu.VMEM((2, WINDOWS, 128 * QUAD), f32),
            pltpu.VMEM((2, WINDOWS, 128 * QUAD), f32),
            pltpu.VMEM((TEMPL, 256, 128), f32),
            pltpu.VMEM((TEMPL, 384, 128), f32),
            pltpu.VMEM((2, 4, 512, 128), f32),
            pltpu.SemaphoreType.DMA((QUADS - 1,)),
            pltpu.SemaphoreType.DMA((2, 4)),
        ],
        compiler_params=grant(50),
        name="power",
    )(sub_rows, arrived, head, rest, jnp.asarray(spread_matrices()))
    return summed.reshape(2, 256, 8, LANES).transpose(0, 2, 1, 3).reshape(TEMPL, 256 * LANES)


def solution(mesh):
    in_specs = (P(("dm", "freq")), P(), P(), P())
    out_specs = P(None, ("dm", "freq"))
    return jax.shard_map(
        on_device, mesh=mesh, in_specs=in_specs, out_specs=out_specs, check_vma=False
    )
```

```python
import math

import jax
import jax.numpy as jnp
import numpy as np
from jax import lax
from jax.experimental import pallas as pl
from jax.experimental.pallas import tpu as pltpu
from jax.sharding import PartitionSpec as P

SAMPLES = 4194304
TEMPL = 16
MAXHALF = 64
MEMBERS = 64
LANES = 128
ROWS_OUT = 21

f32 = jnp.float32
bf16 = jnp.bfloat16

MAIN, HALF2, HALF3, HALF1 = 0, 1, 2, 3
COUNTS = (256, 128, 192, 64)
BASES = (0, 264, 400, 600)
GATHERED = 672
WINDOWS = 640
QUAD = 4
QUADS = TEMPL // QUAD


def unit(product, length):
    angles = np.asarray(product, np.float64) % length * (-2.0 * math.pi / length)
    return np.cos(angles), np.sin(angles)


def first_matrix():
    matrix = np.zeros((128, 128))
    wide = np.arange(128)
    for k0 in range(64):
        real, imag = unit(k0 * wide, 128)
        matrix[2 * k0] = real
        matrix[2 * k0 + 1] = imag
    matrix[1] = unit(64 * wide, 128)[0]
    return matrix.astype(np.float32)


def row_order():
    at = np.arange(256)
    return 4 * (at % 64) + at // 64


def second_matrix():
    q, a = np.arange(256)[:, None], row_order()[None, :]
    real, imag = unit(q * a, 256)
    return np.block([[real, -imag], [imag, real]]).astype(np.float32)


def middle_twiddle():
    q, b = np.arange(256)[:, None], np.arange(128)[None, :]
    real, imag = unit(q * b, 32768)
    return np.stack([real, imag]).astype(np.float32)


def third_matrix():
    c, b = np.arange(72)[:, None], np.arange(128)[None, :]
    real, imag = unit(c * b, 128)
    norm = 1.0 / math.sqrt(SAMPLES)
    return (np.block([[real, -imag], [imag, real]]) * norm).astype(np.float32)


def spread_matrices():
    lane, s = np.arange(128)[:, None], np.arange(128)[None, :]
    pairs = []
    for pair in range(2):
        columns = []
        for u in range(2):
            beta = 2 * pair + u
            pieces = [lane == 64 * u + s // 2]
            for v in (pair, pair + 1):
                pieces.append(128 * v + lane == 96 * beta + 3 * s // 4)
            columns.append(np.concatenate(pieces))
        pairs.append(np.concatenate(columns, axis=1))
    return np.stack(pairs).astype(bf16)


def flip_matrix():
    at = np.arange(64)
    return ((64 - at[:, None]) % 64 == at[None, :]).astype(bf16)


def halves(values):
    high = values.astype(bf16)
    return high, (values - high.astype(f32)).astype(bf16)


def constant_halves(matrix):
    high = matrix.astype(bf16)
    low = (matrix - high.astype(np.float32)).astype(bf16)
    return jnp.asarray(np.stack([high, low]))


def product(left, right, dims=((1,), (0,))):
    (left_at,), (right_at,) = dims
    return lax.dot_general(
        jnp.concatenate([left[0], left[0], left[1]], axis=left_at),
        jnp.concatenate([right[0], right[1], right[0]], axis=right_at),
        (dims, ((), ())),
        preferred_element_type=f32,
    )


def pack_kernel(series_hbm, out_hbm, held_ref, fetched, stored):
    parts = [(h, pl.ds(16 * at, 16), 4 * h + at) for at in range(4) for h in range(2)]
    fetches = [
        pltpu.make_async_copy(series_hbm.at[h, span], held_ref.at[h, span], fetched.at[slot])
        for h, span, slot in parts
    ]
    stores = [
        pltpu.make_async_copy(held_ref.at[h, span], out_hbm.at[span, h], stored.at[slot])
        for h, span, slot in parts
    ]
    for fetch in fetches:
        fetch.start()
    for fetch, store in zip(fetches, stores):
        fetch.wait()
        store.start()
    for store in stores:
        store.wait()


def tables_kernel(*refs):
    count = len(refs) // 2
    for source, target in zip(refs[:count], refs[count:]):
        target[...] = source[...]


def first_kernel(matrix_ref, x_ref, out_ref):
    samples = jnp.concatenate([x_ref[pl.ds(jj, 128, stride=4), :] for jj in range(4)], axis=1)
    streams = product((matrix_ref[0], matrix_ref[1]), halves(samples))
    for jj in range(4):
        out_ref[pl.ds(jj, 128, stride=4), :] = streams[:, jj * 128 : jj * 128 + 128]


def spectrum_kernel(
    x_ref, turns_ref, second_ref, middle_ref, third_ref, flag_ref, out_ref, lines_ref, wins_ref
):
    real = jnp.concatenate([x_ref[pl.ds(jj, 64, stride=8), :] for jj in range(4)], axis=0)
    imag = jnp.concatenate([x_ref[pl.ds(4 + jj, 64, stride=8), :] for jj in range(4)], axis=0)
    special = flag_ref[0] == 0
    lone = jnp.where(special, imag, real)
    kept = jnp.where(special, jnp.zeros_like(imag), imag)
    at, bt, ct, dt = turns_ref[0], turns_ref[1], turns_ref[2], turns_ref[3]
    stacked = jnp.concatenate(
        [
            jnp.concatenate([real * at - kept * bt, lone * ct - kept * dt], axis=1),
            jnp.concatenate([real * bt + kept * at, -(lone * dt + kept * ct)], axis=1),
        ],
        axis=0,
    )
    stage = product((second_ref[0], second_ref[1]), halves(stacked))
    mid_real, mid_imag = middle_ref[0], middle_ref[1]
    for half in range(2):
        part = stage[:, half * 128 : half * 128 + 128]
        part_real, part_imag = part[:256], part[256:]
        turned = jnp.concatenate(
            [
                part_real * mid_real - part_imag * mid_imag,
                part_real * mid_imag + part_imag * mid_real,
            ],
            axis=1,
        )
        lines = product((third_ref[0], third_ref[1]), halves(turned), ((1,), (1,)))
        c_at = lax.broadcasted_iota(jnp.int32, (72, 256), 0)
        q_at = lax.broadcasted_iota(jnp.int32, (72, 256), 1)
        outside = jnp.logical_and(q_at == 0, c_at == (0 if half else 64))
        for ri in range(2):
            arr = half * 2 + ri
            kept_lines = jnp.where(outside, 0.0, lines[ri * 72 : ri * 72 + 72])
            for tile in range(2):
                lines_ref[arr, tile] = kept_lines[:, tile * 128 : tile * 128 + 128]
    low = lax.broadcasted_iota(jnp.int32, (16, 128), 1) < 64

    def swap(tile):
        return pltpu.roll(tile, 64, 1)

    for arr in range(4):
        for u in range(2):
            wins_ref[arr, u] = lines_ref[arr, u]
            wins_ref[arr, 2, pl.ds(u, 32, stride=2), :] = lines_ref[arr, u, 0:32, :]
        wins_ref[arr, 2, 64:65, :] = lines_ref[arr, 0, 32:33, :]
        t = [
            [lines_ref[arr, w, pl.ds(v, 16, stride=3), :] for w in range(2)]
            for v in range(3)
        ]
        firsts = (
            t[0][0],
            jnp.where(low, swap(t[0][1]), swap(t[1][0])),
            t[1][1],
            jnp.where(low, swap(t[2][0]), swap(t[2][1])),
        )
        seconds = (t[0][1], swap(t[1][0]), t[2][0], swap(t[2][1]))
        s0 = lines_ref[arr, 0, 0:16, :]
        s1 = lines_ref[arr, 1, 0:16, :]
        quarters = (swap(s0), s0, swap(s1), s1)
        for w in range(4):
            wins_ref[arr, 3, pl.ds(w, 16, stride=4), :] = firsts[w]
            wins_ref[arr, 4, pl.ds(w, 16, stride=4), :] = jnp.where(low, seconds[w], quarters[w])
        wins_ref[arr, 3, 64:65, :] = lines_ref[arr, 0, 48:49, :]
        wins_ref[arr, 4, 64:65, :] = pltpu.roll(lines_ref[arr, 0, 16:17, :], 64, 1)
    lane = lax.broadcasted_iota(jnp.int32, (64, 128), 1)
    tails = jnp.zeros((64, 128), f32)
    for arr in range(4):
        for tile in range(5):
            row = arr * 5 + tile
            out_ref[pl.ds(row, 64, stride=ROWS_OUT), :] = wins_ref[arr, tile, 0:64, :]
        for g, (tile, column) in enumerate(((0, 0), (2, 0), (3, 0), (4, 64))):
            value = wins_ref[arr, tile, 1:65, column : column + 1]
            tails = jnp.where(lane == arr * 4 + g, value, tails)
    out_ref[pl.ds(20, 64, stride=ROWS_OUT), :] = tails


def taps_kernel(v_ref, flip_ref, taps_ref):
    natural = [
        jnp.concatenate(
            [
                pltpu.roll(
                    jnp.broadcast_to(v_ref[part, t], (256, 256)), 0, 1, stride=1, stride_axis=0
                )[:, :128]
                for t in range(QUAD)
            ],
            axis=1,
        )
        for part in range(2)
    ]
    trio = (natural[0] + natural[1], natural[0], natural[1])
    for which, matrix in enumerate(trio):
        for level, split in enumerate(halves(matrix)):
            for base in (0, 128):
                taps_ref[0, level, which, base : base + 64] = jnp.dot(
                    flip_ref[...], split[base : base + 64], preferred_element_type=f32
                ).astype(bf16)
                taps_ref[0, level, which, base + 64 : base + 128] = split[
                    base + 64 : base + 128
                ]


def gather(x_ref, gathered_ref, tails, ri):
    lane = lax.broadcasted_iota(jnp.int32, (1, 128), 1)
    for tile in range(5):
        block = jnp.concatenate(
            [
                x_ref[pl.ds((half * 2 + ri) * 5 + tile, 64, stride=ROWS_OUT), :]
                for half in (1, 0)
            ],
            axis=0,
        )
        block = jnp.transpose(block)
        if tile < 2:
            gathered_ref[ri, tile * 128 : tile * 128 + 128] = block
        elif tile == 2:
            gathered_ref[ri, BASES[1] : BASES[1] + 128] = block
        elif tile == 3:
            gathered_ref[ri, BASES[2] : BASES[2] + 128] = block
        else:
            gathered_ref[ri, BASES[2] + 128 : BASES[2] + 192] = block[:64]
            gathered_ref[ri, BASES[3] : BASES[3] + 64] = block[64:]
    for g in range(4):
        upper = tails[(2 + ri) * 4 + g : (2 + ri) * 4 + g + 1]
        lower = tails[ri * 4 + g : ri * 4 + g + 1]
        at = BASES[g] + COUNTS[g]
        gathered_ref[ri, at : at + 1] = jnp.where(lane < 64, upper, lower)


def make_windows(gathered_ref, win_high_ref, win_low_ref, which):
    places = [(beta * 64, beta, 4) for beta in range(4)]
    places += [(256 + v * 64, BASES[1] + v, 2) for v in range(2)]
    places += [(384 + v * 64, BASES[2] + v, 3) for v in range(3)]
    places += [(576, BASES[3], 1)]
    for target, source, stride in places:
        for shift in range(2):
            values = gathered_ref[0, pl.ds(source + shift, 64, stride=stride), :]
            if which:
                imag = gathered_ref[1, pl.ds(source + shift, 64, stride=stride), :]
                values = imag - values if which == 1 else imag + values
            span = slice(shift * 128, shift * 128 + 128)
            high, low = halves(values)
            win_high_ref[which, target : target + 64, span] = high
            win_low_ref[which, target : target + 64, span] = low


def power_kernel(
    rows_ref,
    x_ref,
    head_ref,
    rest_hbm,
    spread_ref,
    out_hbm,
    gathered_ref,
    win_high_ref,
    win_low_ref,
    rest_ref,
    parts_ref,
    squares_ref,
    sum_ref,
    lower_ref,
    out_ref,
    fetched,
    stored,
):
    fetches = [
        pltpu.make_async_copy(rest_hbm.at[at], rest_ref.at[at], fetched.at[at])
        for at in range(QUADS - 1)
    ]
    for fetch in fetches:
        fetch.start()
    tails = x_ref[pl.ds(20, 64, stride=ROWS_OUT), :]
    tails = jnp.transpose(jnp.concatenate([tails, tails], axis=0))
    gather(x_ref, gathered_ref, tails, 0)
    make_windows(gathered_ref, win_high_ref, win_low_ref, 0)

    for quad in range(QUADS):
        taps_ref, at_quad = (rest_ref, quad - 1) if quad else (head_ref, 0)

        def part(which):
            return product(
                (win_high_ref[which], win_low_ref[which]),
                (taps_ref[at_quad, 0, which], taps_ref[at_quad, 1, which]),
            )

        slot = quad % 2
        parts_ref[slot] = part(0)
        if quad == 0:
            gather(x_ref, gathered_ref, tails, 1)
            make_windows(gathered_ref, win_high_ref, win_low_ref, 1)
            make_windows(gathered_ref, win_high_ref, win_low_ref, 2)
        imag = parts_ref[slot] + part(1)
        squares_ref[slot] = imag * imag
        if quad == 0:
            for fetch in fetches:
                fetch.wait()
        real = parts_ref[slot] - part(2)
        power = real * real + squares_ref[slot]
        for at in range(QUAD):
            t = quad * QUAD + at
            span = slice(at * 128, at * 128 + 128)
            sum_ref[t] = power[:256, span]
            lower_ref[t] = power[256:, span]

    lane = lax.broadcasted_iota(jnp.int32, (64, 128), 1)
    stores = []
    for chunk in range(2):
        first = chunk * 8
        places = ((1, 0), (1, 64), (2, 128), (2, 192), (2, 256))
        sources = [
            jnp.concatenate(
                halves(
                    jnp.concatenate(
                        [lower_ref[rows_ref[h, first + t], at : at + 64] for t in range(8)], axis=0
                    )
                ),
                axis=1,
            )
            for h, at in places
        ]
        for pair in range(2):
            spread = jnp.dot(
                jnp.concatenate([sources[pair], sources[2 + pair], sources[3 + pair]], axis=1),
                jnp.concatenate(
                    [spread_ref[pair, 128 * (k // 2) : 128 * (k // 2) + 128] for k in range(6)],
                    axis=0,
                ),
                preferred_element_type=f32,
            )
            for u in range(2):
                beta = 2 * pair + u
                for t in range(8):
                    singles = jnp.take_along_axis(
                        lower_ref[rows_ref[0, first + t], 320:384],
                        32 * beta + lane // 4,
                        axis=1,
                        mode="promise_in_bounds",
                    )
                    out_ref[chunk, beta, pl.ds(t, 64, stride=8), :] = (
                        sum_ref[first + t, beta * 64 : beta * 64 + 64]
                        + singles
                        + spread[t * 64 : t * 64 + 64, u * 128 : u * 128 + 128]
                    )
                stores.append(
                    pltpu.make_async_copy(
                        out_ref.at[chunk, beta].reshape(64, 8, 128),
                        out_hbm.at[chunk, :, beta],
                        stored.at[chunk, beta],
                    )
                )
                if chunk + pair == 2:
                    stores[-1].start()
            if chunk + pair < 2:
                for store in stores[-2:]:
                    store.start()
    for store in stores:
        store.wait()


def swap_blocks(values):
    return lax.all_to_all(values, "freq", split_axis=0, concat_axis=0, tiled=True)


def turn_tables(position):
    m = 128 * jnp.asarray(row_order(), jnp.int32)[:, None] + jnp.arange(128, dtype=jnp.int32)
    tables = []
    for residue in (position, jnp.where(position == 0, 64, position)):
        angles = (m * residue).astype(f32) * (-2.0 * math.pi / SAMPLES)
        tables += [jnp.cos(angles), jnp.sin(angles)]
    return jnp.stack(tables)


def tap_rows(kernels, half_widths):
    offsets = jnp.abs(jnp.arange(2 * MAXHALF + 1, dtype=jnp.int32) - MAXHALF)
    inside = offsets[None, :] <= half_widths[:, None]
    taps = jnp.where(inside[None], kernels, 0.0)
    return jnp.concatenate(
        [taps[:, :, 0:1], jnp.zeros((2, TEMPL, 127), f32), taps[:, :, :0:-1]], axis=2
    ).reshape(2, TEMPL, 1, 256)


def whole(shape):
    return pl.BlockSpec(shape, lambda i: (0,) * len(shape))


def grant(mebibytes):
    return pltpu.CompilerParams(
        vmem_limit_bytes=mebibytes << 20
    )


def on_device(series, kernels, half_widths, sub_rows):
    position = lax.axis_index("freq")
    blocks = pl.pallas_call(
        pack_kernel,
        in_specs=[pl.BlockSpec(memory_space=pltpu.HBM)],
        out_specs=pl.BlockSpec(memory_space=pltpu.HBM),
        out_shape=jax.ShapeDtypeStruct((MEMBERS, 2, 4, LANES), f32),
        scratch_shapes=[
            pltpu.VMEM((2, MEMBERS, 4, LANES), f32),
            pltpu.SemaphoreType.DMA((8,)),
            pltpu.SemaphoreType.DMA((8,)),
        ],
        name="pack",
    )(series.reshape(2, MEMBERS, 4, LANES))
    arrived = swap_blocks(blocks).reshape(512, LANES)
    tables = (
        constant_halves(first_matrix()),
        constant_halves(second_matrix()),
        jnp.asarray(middle_twiddle()),
        constant_halves(third_matrix()),
    )
    first, second, middle, third = pl.pallas_call(
        tables_kernel,
        out_shape=[jax.ShapeDtypeStruct(table.shape, table.dtype) for table in tables],
        compiler_params=grant(12),
        name="tables",
    )(*tables)
    streams = pl.pallas_call(
        first_kernel,
        in_specs=[pl.BlockSpec(memory_space=pltpu.VMEM)] * 2,
        out_shape=jax.ShapeDtypeStruct((512, LANES), f32),
        compiler_params=grant(4),
        name="first",
    )(first, arrived)
    arrived = swap_blocks(streams)
    outgoing = pl.pallas_call(
        spectrum_kernel,
        in_specs=[pl.BlockSpec(memory_space=pltpu.VMEM)] * 5 + [pl.BlockSpec(memory_space=pltpu.SMEM)],
        out_shape=jax.ShapeDtypeStruct((MEMBERS * ROWS_OUT, LANES), f32),
        scratch_shapes=[pltpu.VMEM((4, 2, 72, 128), f32), pltpu.VMEM((4, 5, 72, 128), f32)],
        compiler_params=grant(12),
        name="spectrum",
    )(
        arrived,
        turn_tables(position),
        second,
        middle,
        third,
        position.reshape(1),
    )
    outgoing = outgoing.reshape(MEMBERS, ROWS_OUT, 1, LANES)
    arrived = swap_blocks(outgoing).reshape(MEMBERS * ROWS_OUT, LANES)
    taps_shape = (2, 3, 256, 128 * QUAD)
    rows = tap_rows(kernels, half_widths)
    flip = jnp.asarray(flip_matrix())

    def taps(start, count, mebibytes):
        return pl.pallas_call(
            taps_kernel,
            grid=(count,),
            in_specs=[
                pl.BlockSpec((2, QUAD, 1, 256), lambda i: (0, i + start, 0, 0)),
                whole((64, 64)),
            ],
            out_specs=pl.BlockSpec((1, *taps_shape), lambda i: (i, 0, 0, 0, 0)),
            out_shape=jax.ShapeDtypeStruct((count, *taps_shape), bf16),
            compiler_params=grant(mebibytes),
            name="taps",
        )(rows, flip)

    head, rest = taps(0, 1, 10), taps(1, QUADS - 1, 58)
    summed = pl.pallas_call(
        power_kernel,
        in_specs=[
            pl.BlockSpec(memory_space=pltpu.SMEM),
            pl.BlockSpec(memory_space=pltpu.VMEM),
            pl.BlockSpec(memory_space=pltpu.VMEM),
            pl.BlockSpec(memory_space=pltpu.HBM),
            pl.BlockSpec(memory_space=pltpu.VMEM),
        ],
        out_specs=pl.BlockSpec(memory_space=pltpu.HBM),
        out_shape=jax.ShapeDtypeStruct((2, 64, 4, 8, LANES), f32),
        scratch_shapes=[
            pltpu.VMEM((2, GATHERED, 128), f32),
            pltpu.VMEM((3, WINDOWS, 256), bf16),
            pltpu.VMEM((3, WINDOWS, 256), bf16),
            pltpu.VMEM((QUADS - 1, *taps_shape), bf16),
            pltpu.VMEM((2, WINDOWS, 128 * QUAD), f32),
            pltpu.VMEM((2, WINDOWS, 128 * QUAD), f32),
            pltpu.VMEM((TEMPL, 256, 128), f32),
            pltpu.VMEM((TEMPL, 384, 128), f32),
            pltpu.VMEM((2, 4, 512, 128), f32),
            pltpu.SemaphoreType.DMA((QUADS - 1,)),
            pltpu.SemaphoreType.DMA((2, 4)),
        ],
        compiler_params=grant(50),
        name="power",
    )(sub_rows, arrived, head, rest, jnp.asarray(spread_matrices()))
    return summed.reshape(2, 256, 8, LANES).transpose(0, 2, 1, 3).reshape(TEMPL, 256 * LANES)


def solution(mesh):
    in_specs = (P(("dm", "freq")), P(), P(), P())
    out_specs = P(None, ("dm", "freq"))
    return jax.shard_map(
        on_device, mesh=mesh, in_specs=in_specs, out_specs=out_specs, check_vma=False
    )
```

```python
import math

import jax
import jax.numpy as jnp
import numpy as np
from jax import lax
from jax.experimental import pallas as pl
from jax.experimental.pallas import tpu as pltpu
from jax.sharding import PartitionSpec as P

SAMPLES = 4194304
TEMPL = 16
MAXHALF = 64
MEMBERS = 64
LANES = 128
ROWS_OUT = 21

f32 = jnp.float32
bf16 = jnp.bfloat16

MAIN, HALF2, HALF3, HALF1 = 0, 1, 2, 3
COUNTS = (256, 128, 192, 64)
BASES = (0, 264, 400, 600)
GATHERED = 672
WINDOWS = 640
QUAD = 4
QUADS = TEMPL // QUAD


def unit(product, length):
    angles = np.asarray(product, np.float64) % length * (-2.0 * math.pi / length)
    return np.cos(angles), np.sin(angles)


def first_matrix():
    matrix = np.zeros((128, 128))
    wide = np.arange(128)
    for k0 in range(64):
        real, imag = unit(k0 * wide, 128)
        matrix[2 * k0] = real
        matrix[2 * k0 + 1] = imag
    matrix[1] = unit(64 * wide, 128)[0]
    return matrix.astype(np.float32)


def row_order():
    at = np.arange(256)
    return 4 * (at % 64) + at // 64


def second_matrix():
    q, a = np.arange(256)[:, None], row_order()[None, :]
    real, imag = unit(q * a, 256)
    return np.block([[real, -imag], [imag, real]]).astype(np.float32)


def middle_twiddle():
    q, b = np.arange(256)[:, None], np.arange(128)[None, :]
    real, imag = unit(q * b, 32768)
    return np.stack([real, imag]).astype(np.float32)


def third_matrix():
    c, b = np.arange(72)[:, None], np.arange(128)[None, :]
    real, imag = unit(c * b, 128)
    norm = 1.0 / math.sqrt(SAMPLES)
    return (np.block([[real, -imag], [imag, real]]) * norm).astype(np.float32)


def spread_matrices():
    lane, s = np.arange(128)[:, None], np.arange(128)[None, :]
    pairs = []
    for pair in range(2):
        columns = []
        for u in range(2):
            beta = 2 * pair + u
            pieces = [lane == 64 * u + s // 2]
            for v in (pair, pair + 1):
                pieces.append(128 * v + lane == 96 * beta + 3 * s // 4)
            columns.append(np.concatenate(pieces))
        pairs.append(np.concatenate(columns, axis=1))
    return np.stack(pairs).astype(bf16)


def flip_matrix():
    at = np.arange(64)
    return ((64 - at[:, None]) % 64 == at[None, :]).astype(bf16)


def halves(values):
    high = values.astype(bf16)
    return high, (values - high.astype(f32)).astype(bf16)


def constant_halves(matrix):
    high = matrix.astype(bf16)
    low = (matrix - high.astype(np.float32)).astype(bf16)
    return jnp.asarray(np.stack([high, low]))


def product(left, right, dims=((1,), (0,))):
    (left_at,), (right_at,) = dims
    return lax.dot_general(
        jnp.concatenate([left[0], left[0], left[1]], axis=left_at),
        jnp.concatenate([right[0], right[1], right[0]], axis=right_at),
        (dims, ((), ())),
        preferred_element_type=f32,
    )


def pack_kernel(series_hbm, out_hbm, held_ref, fetched, stored):
    parts = [(h, pl.ds(16 * at, 16), 4 * h + at) for at in range(4) for h in range(2)]
    fetches = [
        pltpu.make_async_copy(series_hbm.at[h, span], held_ref.at[h, span], fetched.at[slot])
        for h, span, slot in parts
    ]
    stores = [
        pltpu.make_async_copy(held_ref.at[h, span], out_hbm.at[span, h], stored.at[slot])
        for h, span, slot in parts
    ]
    for fetch in fetches:
        fetch.start()
    for fetch, store in zip(fetches, stores):
        fetch.wait()
        store.start()
    for store in stores:
        store.wait()


def tables_kernel(*refs):
    count = len(refs) // 2
    for source, target in zip(refs[:count], refs[count:]):
        target[...] = source[...]


def first_kernel(matrix_ref, x_ref, out_ref):
    samples = jnp.concatenate([x_ref[pl.ds(jj, 128, stride=4), :] for jj in range(4)], axis=1)
    streams = product((matrix_ref[0], matrix_ref[1]), halves(samples))
    for jj in range(4):
        out_ref[pl.ds(jj, 128, stride=4), :] = streams[:, jj * 128 : jj * 128 + 128]


def spectrum_kernel(
    x_ref, turns_ref, second_ref, middle_ref, third_ref, flag_ref, out_ref, lines_ref, wins_ref
):
    real = jnp.concatenate([x_ref[pl.ds(jj, 64, stride=8), :] for jj in range(4)], axis=0)
    imag = jnp.concatenate([x_ref[pl.ds(4 + jj, 64, stride=8), :] for jj in range(4)], axis=0)
    special = flag_ref[0] == 0
    lone = jnp.where(special, imag, real)
    kept = jnp.where(special, jnp.zeros_like(imag), imag)
    at, bt, ct, dt = turns_ref[0], turns_ref[1], turns_ref[2], turns_ref[3]
    stacked = jnp.concatenate(
        [
            jnp.concatenate([real * at - kept * bt, lone * ct - kept * dt], axis=1),
            jnp.concatenate([real * bt + kept * at, -(lone * dt + kept * ct)], axis=1),
        ],
        axis=0,
    )
    stage = product((second_ref[0], second_ref[1]), halves(stacked))
    mid_real, mid_imag = middle_ref[0], middle_ref[1]
    for half in range(2):
        part = stage[:, half * 128 : half * 128 + 128]
        part_real, part_imag = part[:256], part[256:]
        turned = jnp.concatenate(
            [
                part_real * mid_real - part_imag * mid_imag,
                part_real * mid_imag + part_imag * mid_real,
            ],
            axis=1,
        )
        lines = product((third_ref[0], third_ref[1]), halves(turned), ((1,), (1,)))
        c_at = lax.broadcasted_iota(jnp.int32, (72, 256), 0)
        q_at = lax.broadcasted_iota(jnp.int32, (72, 256), 1)
        outside = jnp.logical_and(q_at == 0, c_at == (0 if half else 64))
        for ri in range(2):
            arr = half * 2 + ri
            kept_lines = jnp.where(outside, 0.0, lines[ri * 72 : ri * 72 + 72])
            for tile in range(2):
                lines_ref[arr, tile] = kept_lines[:, tile * 128 : tile * 128 + 128]
    low = lax.broadcasted_iota(jnp.int32, (16, 128), 1) < 64

    def swap(tile):
        return pltpu.roll(tile, 64, 1)

    for arr in range(4):
        for u in range(2):
            wins_ref[arr, u] = lines_ref[arr, u]
            wins_ref[arr, 2, pl.ds(u, 32, stride=2), :] = lines_ref[arr, u, 0:32, :]
        wins_ref[arr, 2, 64:65, :] = lines_ref[arr, 0, 32:33, :]
        t = [
            [lines_ref[arr, w, pl.ds(v, 16, stride=3), :] for w in range(2)]
            for v in range(3)
        ]
        firsts = (
            t[0][0],
            jnp.where(low, swap(t[0][1]), swap(t[1][0])),
            t[1][1],
            jnp.where(low, swap(t[2][0]), swap(t[2][1])),
        )
        seconds = (t[0][1], swap(t[1][0]), t[2][0], swap(t[2][1]))
        s0 = lines_ref[arr, 0, 0:16, :]
        s1 = lines_ref[arr, 1, 0:16, :]
        quarters = (swap(s0), s0, swap(s1), s1)
        for w in range(4):
            wins_ref[arr, 3, pl.ds(w, 16, stride=4), :] = firsts[w]
            wins_ref[arr, 4, pl.ds(w, 16, stride=4), :] = jnp.where(low, seconds[w], quarters[w])
        wins_ref[arr, 3, 64:65, :] = lines_ref[arr, 0, 48:49, :]
        wins_ref[arr, 4, 64:65, :] = pltpu.roll(lines_ref[arr, 0, 16:17, :], 64, 1)
    lane = lax.broadcasted_iota(jnp.int32, (64, 128), 1)
    tails = jnp.zeros((64, 128), f32)
    for arr in range(4):
        for tile in range(5):
            row = arr * 5 + tile
            out_ref[pl.ds(row, 64, stride=ROWS_OUT), :] = wins_ref[arr, tile, 0:64, :]
        for g, (tile, column) in enumerate(((0, 0), (2, 0), (3, 0), (4, 64))):
            value = wins_ref[arr, tile, 1:65, column : column + 1]
            tails = jnp.where(lane == arr * 4 + g, value, tails)
    out_ref[pl.ds(20, 64, stride=ROWS_OUT), :] = tails


def taps_kernel(v_ref, flip_ref, taps_ref):
    natural = [
        jnp.concatenate(
            [
                pltpu.roll(
                    jnp.broadcast_to(v_ref[part, t], (256, 256)), 0, 1, stride=1, stride_axis=0
                )[:, :128]
                for t in range(QUAD)
            ],
            axis=1,
        )
        for part in range(2)
    ]
    trio = (natural[0] + natural[1], natural[0], natural[1])
    for which, matrix in enumerate(trio):
        for level, split in enumerate(halves(matrix)):
            for base in (0, 128):
                taps_ref[0, level, which, base : base + 64] = jnp.dot(
                    flip_ref[...], split[base : base + 64], preferred_element_type=f32
                ).astype(bf16)
                taps_ref[0, level, which, base + 64 : base + 128] = split[
                    base + 64 : base + 128
                ]


def gather(x_ref, gathered_ref, tails, ri):
    lane = lax.broadcasted_iota(jnp.int32, (1, 128), 1)
    for tile in range(5):
        block = jnp.concatenate(
            [
                x_ref[pl.ds((half * 2 + ri) * 5 + tile, 64, stride=ROWS_OUT), :]
                for half in (1, 0)
            ],
            axis=0,
        )
        block = jnp.transpose(block)
        if tile < 2:
            gathered_ref[ri, tile * 128 : tile * 128 + 128] = block
        elif tile == 2:
            gathered_ref[ri, BASES[1] : BASES[1] + 128] = block
        elif tile == 3:
            gathered_ref[ri, BASES[2] : BASES[2] + 128] = block
        else:
            gathered_ref[ri, BASES[2] + 128 : BASES[2] + 192] = block[:64]
            gathered_ref[ri, BASES[3] : BASES[3] + 64] = block[64:]
    for g in range(4):
        upper = tails[(2 + ri) * 4 + g : (2 + ri) * 4 + g + 1]
        lower = tails[ri * 4 + g : ri * 4 + g + 1]
        at = BASES[g] + COUNTS[g]
        gathered_ref[ri, at : at + 1] = jnp.where(lane < 64, upper, lower)


def make_windows(gathered_ref, win_high_ref, win_low_ref, which):
    places = [(beta * 64, beta, 4) for beta in range(4)]
    places += [(256 + v * 64, BASES[1] + v, 2) for v in range(2)]
    places += [(384 + v * 64, BASES[2] + v, 3) for v in range(3)]
    places += [(576, BASES[3], 1)]
    for target, source, stride in places:
        for shift in range(2):
            values = gathered_ref[0, pl.ds(source + shift, 64, stride=stride), :]
            if which:
                imag = gathered_ref[1, pl.ds(source + shift, 64, stride=stride), :]
                values = imag - values if which == 1 else imag + values
            span = slice(shift * 128, shift * 128 + 128)
            high, low = halves(values)
            win_high_ref[which, target : target + 64, span] = high
            win_low_ref[which, target : target + 64, span] = low


def power_kernel(
    rows_ref,
    x_ref,
    head_ref,
    rest_hbm,
    spread_ref,
    out_hbm,
    gathered_ref,
    win_high_ref,
    win_low_ref,
    rest_ref,
    parts_ref,
    squares_ref,
    sum_ref,
    lower_ref,
    out_ref,
    fetched,
    stored,
):
    fetches = [
        pltpu.make_async_copy(rest_hbm.at[at], rest_ref.at[at], fetched.at[at])
        for at in range(QUADS - 1)
    ]
    for fetch in fetches:
        fetch.start()
    tails = x_ref[pl.ds(20, 64, stride=ROWS_OUT), :]
    tails = jnp.transpose(jnp.concatenate([tails, tails], axis=0))
    gather(x_ref, gathered_ref, tails, 0)
    make_windows(gathered_ref, win_high_ref, win_low_ref, 0)

    for quad in range(QUADS):
        taps_ref, at_quad = (rest_ref, quad - 1) if quad else (head_ref, 0)

        def part(which):
            return product(
                (win_high_ref[which], win_low_ref[which]),
                (taps_ref[at_quad, 0, which], taps_ref[at_quad, 1, which]),
            )

        slot = quad % 2
        parts_ref[slot] = part(0)
        if quad == 0:
            gather(x_ref, gathered_ref, tails, 1)
            make_windows(gathered_ref, win_high_ref, win_low_ref, 1)
            make_windows(gathered_ref, win_high_ref, win_low_ref, 2)
        imag = parts_ref[slot] + part(1)
        squares_ref[slot] = imag * imag
        if quad == 0:
            for fetch in fetches:
                fetch.wait()
        real = parts_ref[slot] - part(2)
        power = real * real + squares_ref[slot]
        for at in range(QUAD):
            t = quad * QUAD + at
            span = slice(at * 128, at * 128 + 128)
            sum_ref[t] = power[:256, span]
            lower_ref[t] = power[256:, span]

    lane = lax.broadcasted_iota(jnp.int32, (64, 128), 1)
    stores = []
    for chunk in range(2):
        first = chunk * 8
        places = ((1, 0), (1, 64), (2, 128), (2, 192), (2, 256))
        sources = [
            jnp.concatenate(
                halves(
                    jnp.concatenate(
                        [lower_ref[rows_ref[h, first + t], at : at + 64] for t in range(8)], axis=0
                    )
                ),
                axis=1,
            )
            for h, at in places
        ]
        for pair in range(2):
            final = chunk + pair == 2
            for begin in (0, 4) if final else (0,):
                count = 4 if final else 8
                spread = jnp.dot(
                    jnp.concatenate(
                        [
                            sources[at][begin * 64 : (begin + count) * 64]
                            for at in (pair, 2 + pair, 3 + pair)
                        ],
                        axis=1,
                    ),
                    jnp.concatenate(
                        [spread_ref[pair, 128 * (k // 2) : 128 * (k // 2) + 128] for k in range(6)],
                        axis=0,
                    ),
                    preferred_element_type=f32,
                )
                for u in range(2):
                    beta = 2 * pair + u
                    for at in range(count):
                        t = begin + at
                        singles = jnp.take_along_axis(
                            lower_ref[rows_ref[0, first + t], 320:384],
                            32 * beta + lane // 4,
                            axis=1,
                            mode="promise_in_bounds",
                        )
                        out_ref[chunk, beta, pl.ds(t, 64, stride=8), :] = (
                            sum_ref[first + t, beta * 64 : beta * 64 + 64]
                            + singles
                            + spread[at * 64 : at * 64 + 64, u * 128 : u * 128 + 128]
                        )
                    if begin + count == 8:
                        stores.append(
                            pltpu.make_async_copy(
                                out_ref.at[chunk, beta].reshape(64, 8, 128),
                                out_hbm.at[chunk, :, beta],
                                stored.at[chunk, beta],
                            )
                        )
                        if final:
                            stores[-1].start()
            if not final:
                for store in stores[-2:]:
                    store.start()
    for store in stores:
        store.wait()


def swap_blocks(values):
    return lax.all_to_all(values, "freq", split_axis=0, concat_axis=0, tiled=True)


def turn_tables(position):
    m = 128 * jnp.asarray(row_order(), jnp.int32)[:, None] + jnp.arange(128, dtype=jnp.int32)
    tables = []
    for residue in (position, jnp.where(position == 0, 64, position)):
        angles = (m * residue).astype(f32) * (-2.0 * math.pi / SAMPLES)
        tables += [jnp.cos(angles), jnp.sin(angles)]
    return jnp.stack(tables)


def tap_rows(kernels, half_widths):
    offsets = jnp.abs(jnp.arange(2 * MAXHALF + 1, dtype=jnp.int32) - MAXHALF)
    inside = offsets[None, :] <= half_widths[:, None]
    taps = jnp.where(inside[None], kernels, 0.0)
    return jnp.concatenate(
        [taps[:, :, 0:1], jnp.zeros((2, TEMPL, 127), f32), taps[:, :, :0:-1]], axis=2
    ).reshape(2, TEMPL, 1, 256)


def whole(shape):
    return pl.BlockSpec(shape, lambda i: (0,) * len(shape))


def grant(mebibytes):
    return pltpu.CompilerParams(
        vmem_limit_bytes=mebibytes << 20
    )


def on_device(series, kernels, half_widths, sub_rows):
    position = lax.axis_index("freq")
    blocks = pl.pallas_call(
        pack_kernel,
        in_specs=[pl.BlockSpec(memory_space=pltpu.HBM)],
        out_specs=pl.BlockSpec(memory_space=pltpu.HBM),
        out_shape=jax.ShapeDtypeStruct((MEMBERS, 2, 4, LANES), f32),
        scratch_shapes=[
            pltpu.VMEM((2, MEMBERS, 4, LANES), f32),
            pltpu.SemaphoreType.DMA((8,)),
            pltpu.SemaphoreType.DMA((8,)),
        ],
        name="pack",
    )(series.reshape(2, MEMBERS, 4, LANES))
    arrived = swap_blocks(blocks).reshape(512, LANES)
    tables = (
        constant_halves(first_matrix()),
        constant_halves(second_matrix()),
        jnp.asarray(middle_twiddle()),
        constant_halves(third_matrix()),
    )
    first, second, middle, third = pl.pallas_call(
        tables_kernel,
        out_shape=[jax.ShapeDtypeStruct(table.shape, table.dtype) for table in tables],
        compiler_params=grant(12),
        name="tables",
    )(*tables)
    streams = pl.pallas_call(
        first_kernel,
        in_specs=[pl.BlockSpec(memory_space=pltpu.VMEM)] * 2,
        out_shape=jax.ShapeDtypeStruct((512, LANES), f32),
        compiler_params=grant(4),
        name="first",
    )(first, arrived)
    arrived = swap_blocks(streams)
    outgoing = pl.pallas_call(
        spectrum_kernel,
        in_specs=[pl.BlockSpec(memory_space=pltpu.VMEM)] * 5 + [pl.BlockSpec(memory_space=pltpu.SMEM)],
        out_shape=jax.ShapeDtypeStruct((MEMBERS * ROWS_OUT, LANES), f32),
        scratch_shapes=[pltpu.VMEM((4, 2, 72, 128), f32), pltpu.VMEM((4, 5, 72, 128), f32)],
        compiler_params=grant(12),
        name="spectrum",
    )(
        arrived,
        turn_tables(position),
        second,
        middle,
        third,
        position.reshape(1),
    )
    outgoing = outgoing.reshape(MEMBERS, ROWS_OUT, 1, LANES)
    arrived = swap_blocks(outgoing).reshape(MEMBERS * ROWS_OUT, LANES)
    taps_shape = (2, 3, 256, 128 * QUAD)
    rows = tap_rows(kernels, half_widths)
    flip = jnp.asarray(flip_matrix())

    def taps(start, count, mebibytes):
        return pl.pallas_call(
            taps_kernel,
            grid=(count,),
            in_specs=[
                pl.BlockSpec((2, QUAD, 1, 256), lambda i: (0, i + start, 0, 0)),
                whole((64, 64)),
            ],
            out_specs=pl.BlockSpec((1, *taps_shape), lambda i: (i, 0, 0, 0, 0)),
            out_shape=jax.ShapeDtypeStruct((count, *taps_shape), bf16),
            compiler_params=grant(mebibytes),
            name="taps",
        )(rows, flip)

    head, rest = taps(0, 1, 10), taps(1, QUADS - 1, 58)
    summed = pl.pallas_call(
        power_kernel,
        in_specs=[
            pl.BlockSpec(memory_space=pltpu.SMEM),
            pl.BlockSpec(memory_space=pltpu.VMEM),
            pl.BlockSpec(memory_space=pltpu.VMEM),
            pl.BlockSpec(memory_space=pltpu.HBM),
            pl.BlockSpec(memory_space=pltpu.VMEM),
        ],
        out_specs=pl.BlockSpec(memory_space=pltpu.HBM),
        out_shape=jax.ShapeDtypeStruct((2, 64, 4, 8, LANES), f32),
        scratch_shapes=[
            pltpu.VMEM((2, GATHERED, 128), f32),
            pltpu.VMEM((3, WINDOWS, 256), bf16),
            pltpu.VMEM((3, WINDOWS, 256), bf16),
            pltpu.VMEM((QUADS - 1, *taps_shape), bf16),
            pltpu.VMEM((2, WINDOWS, 128 * QUAD), f32),
            pltpu.VMEM((2, WINDOWS, 128 * QUAD), f32),
            pltpu.VMEM((TEMPL, 256, 128), f32),
            pltpu.VMEM((TEMPL, 384, 128), f32),
            pltpu.VMEM((2, 4, 512, 128), f32),
            pltpu.SemaphoreType.DMA((QUADS - 1,)),
            pltpu.SemaphoreType.DMA((2, 4)),
        ],
        compiler_params=grant(50),
        name="power",
    )(sub_rows, arrived, head, rest, jnp.asarray(spread_matrices()))
    return summed.reshape(2, 256, 8, LANES).transpose(0, 2, 1, 3).reshape(TEMPL, 256 * LANES)


def solution(mesh):
    in_specs = (P(("dm", "freq")), P(), P(), P())
    out_specs = P(None, ("dm", "freq"))
    return jax.shard_map(
        on_device, mesh=mesh, in_specs=in_specs, out_specs=out_specs, check_vma=False
    )
```
